32 devices in a mesh: mem: 4 (over y, x), space: 8 (over z, core).
Axes of the slice: x: 2, y: 2, z: 4, core: 2. Of those that a mesh axis runs over, the one named last changes fastest.
Arguments:
- state: float32 [16, 5, 64, 16, 256], P('mem', None, 'space'), may hold values from -6 to 6
- diffusion: float32 [5], replicated, may hold values from 0.1 to 0.5
- radius: int32 [16], replicated, may hold values from 4 to 8, as said below
- obs_cells: int32 [8, 128], P('space'), may hold values from 0 to 2047
- obs_count: int32 [8], P('space'), may hold values from 1 to 128, as said below
- obs_value: float32 [8, 128], P('space'), may hold values from -4 to 12
- obs_error: float32 [8, 128], P('space'), may hold values from 0.5 to 2
Outputs:
- analysis: float32 [16, 5, 64, 16, 256], P('mem', None, 'space')
The draws below stay inside these ranges and needn't reach their ends.
Inputs may be any that keep to these rules, and one draw needn't show every extreme that they name: Some level has radius exactly 8. Only the first obs_count[t] entries of a tile's lists are sites; some tile has exactly 128 sites.
All inputs are finite; a program needn't handle non-finite values.
Results may differ from the reference program's by a relative error of at most 0.0003.
Values sent between devices are 32-bit elements; how exact they have to be, the bound alone decides.
A program may use at most 64 MiB of HBM per device.

```python
import math
import jax
import jax.numpy as jnp
from jax import lax

F = 5
CX = 8
NY = 256
NZ = 16
OBS_MAX = 128
MEMBERS = 16
TILES = 8
NX = 64


def draw_radius(key, part):
    key_one, key_two = jax.random.split(jax.random.fold_in(key, 11))
    levels = jax.random.randint(key_one, (NZ,), CX // 2, CX + 1, dtype=jnp.int32)
    chosen = jax.random.randint(key_two, (), 0, NZ, dtype=jnp.int32)
    return jnp.where(jnp.arange(NZ, dtype=jnp.int32) == chosen, CX, levels).astype(jnp.int32)


def draw_obs_count(key, part):
    key_one, key_two = jax.random.split(jax.random.fold_in(key, 23))
    counts = jax.random.randint(key_one, (TILES,), 1, OBS_MAX + 1, dtype=jnp.int32)
    chosen = jax.random.randint(key_two, (), 0, TILES, dtype=jnp.int32)
    return jnp.where(jnp.arange(TILES, dtype=jnp.int32) == chosen, OBS_MAX, counts).astype(jnp.int32)


def draw_obs_value(key, part):
    key_one = jax.random.fold_in(jax.random.fold_in(key, 37), 0)
    noise = jnp.clip(jax.random.normal(key_one, (TILES, OBS_MAX), jnp.float32), -4.0, 4.0)
    return noise.astype(jnp.float32)


def set_ends(drawn, rng, low, top_value):
    longest = drawn.shape.index(max(drawn.shape))
    spots = []
    for shift in (0, 1):
        where = [jax.random.randint(jax.random.fold_in(rng, axis), (), 0, length) for axis, length in enumerate(drawn.shape)]
        where[longest] = (where[longest] + shift) % drawn.shape[longest]
        spots.append(tuple(where))
    return drawn.at[spots[0]].set(low).at[spots[1]].set(top_value)


def steps_of(stream_key, extent, cuts, low, top_value):
    level = 1.0
    for axis_at, parts in cuts:
        steps = jax.random.uniform(jax.random.fold_in(jax.random.fold_in(stream_key, 6), axis_at), (parts,), jnp.float32, low / len(cuts), top_value / len(cuts))
        level = level * jnp.repeat(jnp.exp(steps), extent[axis_at] // parts).reshape((-1,) + (1,) * (len(extent) - 1 - axis_at))
    return level


def centred(key, shape, scale, bound, shards=(), kind=jnp.bfloat16):
    result = jax.random.normal(key, shape, jnp.float32) * scale
    if len(shards) > 0:
        result = steps_of(key, shape, shards, -0.22, 0.18) * result
    return jnp.clip(result, min=-bound, max=bound).astype(kind)


def setup_inputs(seed: int = 0) -> dict:
    keys = jax.random.split(jax.random.key(seed), 8)
    return {
        "state": centred(keys[0], (MEMBERS, F, NX, NZ, NY), 1.0, 6.0, ((0, 4), (2, 8)), jnp.float32),
        "diffusion": jnp.clip(jnp.exp(jax.random.uniform(keys[1], (F,), jnp.float32, math.log(0.1), math.log(0.5))), 0.1, 0.5),
        "radius": draw_radius(jax.random.fold_in(keys[7], 71), 0),
        "obs_cells": set_ends(jax.random.randint(keys[3], (TILES, OBS_MAX), 0, CX * NY), jax.random.fold_in(keys[3], 1), 0, (CX * NY) - 1).astype(jnp.int32),
        "obs_count": draw_obs_count(jax.random.fold_in(keys[7], 71), 0),
        "obs_value": draw_obs_value(jax.random.fold_in(keys[7], 71), 0),
        "obs_error": jnp.clip(jnp.exp(math.log(2.0) - 1.3862944 * jax.random.uniform(keys[6], (TILES, OBS_MAX), jnp.float32) ** steps_of(keys[6], (TILES, OBS_MAX), ((0, 8),), -0.2, 0.2)), 0.5, 2.0),
    }


time_step = 0.2
blend_share = 0.5


def advance(padded, diffuse_rate):
    interior = padded[..., 1:-1, :, :]
    east_side = padded[..., 2:, :, :]
    west_side = padded[..., :-2, :, :]
    north_side = jnp.roll(interior, -1, axis=-1)
    south_side = jnp.roll(interior, 1, axis=-1)
    wind_east = interior[..., 0:1, :, :, :]
    wind_north = interior[..., 1:2, :, :, :]
    transport = wind_east * (east_side - west_side) * 0.5 + wind_north * (north_side - south_side) * 0.5
    spread = east_side + west_side + north_side + south_side - 4.0 * interior
    return interior + time_step * (diffuse_rate * spread - transport)


def tile_weights(misfit3, x_sites, y_sites, inverse):
    cell_index = jnp.arange(CX * NY, dtype=jnp.int32)
    cell_east = cell_index // NY
    cell_north = cell_index % NY
    delta_east = cell_east[:, None] - x_sites[None, :]
    delta_north = (cell_north[:, None] - y_sites[None, :] + NY // 2) % NY - NY // 2
    distance_sq = (delta_east * delta_east + delta_north * delta_north).astype(jnp.float32)

    def level_weights(inverse_level):
        taper = jnp.maximum(0.0, 1.0 - distance_sq * inverse_level) ** 2
        return -0.5 * jnp.einsum("mo,co->mc", misfit3, taper, precision=lax.Precision.HIGHEST)

    return lax.map(level_weights, inverse)


def reference(state, diffusion, radius, obs_cells, obs_count, obs_value, obs_error):
    diffuse_rate = diffusion.reshape(F, 1, 1, 1)

    def evolve(member):
        for sweep_index in range(2):
            padded = jnp.concatenate([member[..., -1:, :, :], member, member[..., :1, :, :]], axis=-3)
            member = advance(padded, diffuse_rate)
        return member

    advected = lax.map(evolve, state)
    column = jnp.mean(advected[:, 2], axis=2)
    column_tiles = column.reshape(MEMBERS, TILES, CX * NY)
    observed = jnp.take_along_axis(column_tiles, obs_cells[None, :, :], axis=2)
    innovation = obs_value[None, :, :] - observed
    is_valid = (jnp.arange(OBS_MAX, dtype=jnp.int32)[None, :] < obs_count[:, None]).astype(jnp.float32)
    misfit = is_valid[None] * (innovation * innovation) / (obs_error * obs_error)[None]
    radius_float = radius.astype(jnp.float32)
    inverse = 1.0 / (radius_float * radius_float)
    offsets = jnp.arange(3, dtype=jnp.int32) - 1

    def one_tile(tile_index):
        neighbour = (tile_index + offsets) % TILES
        misfit3 = misfit[:, neighbour, :].reshape(MEMBERS, 3 * OBS_MAX)
        cells3 = obs_cells[neighbour]
        x_sites = (cells3 // NY + offsets[:, None] * CX).reshape(-1)
        y_sites = (cells3 % NY).reshape(-1)
        return tile_weights(misfit3, x_sites, y_sites, inverse)

    per_tile = lax.map(one_tile, jnp.arange(TILES, dtype=jnp.int32))
    per_tile = per_tile.reshape(TILES, NZ, MEMBERS, CX, NY)
    log_weight = per_tile.transpose(2, 0, 3, 1, 4).reshape(MEMBERS, NX, NZ, NY)
    best_log = jnp.max(log_weight, axis=0)
    expo_weight = jnp.exp(log_weight - best_log[None])
    weight_total = jnp.sum(expo_weight, axis=0)
    weighted = jnp.einsum("mxzy,mfxzy->fxzy", expo_weight, advected, precision=lax.Precision.HIGHEST)
    local_mean = weighted / weight_total[None]
    return advected + blend_share * (local_mean[None] - advected)
```

```python
import functools

import jax
import jax.numpy as jnp
from jax import lax
from jax.experimental import pallas as pl
from jax.experimental.pallas import tpu as pltpu
from jax.sharding import PartitionSpec as P

time_step = 0.2
blend_share = 0.5
observed_field = 2
MESH = pl.DeviceIdType.MESH


def distance_classes(reach):
    classes = {}
    for a in range(reach):
        for b in range(reach):
            if a * a + b * b < reach * reach:
                classes.setdefault(a * a + b * b, []).append((a, b))
    return sorted(classes.items())


def kernel(
    n_mem, n_space, dims,
    state, *rest,
):
    small_hbm, rest = rest[:6], rest[6:]
    adv, mean = rest[:2]
    small, rest = rest[2:8], rest[8:]
    (
        st, mid, obs_img, img, rolled, table, classed, gain, part, inbox, share,
        small_sem, load_sem, halo_send, halo_recv, img_send, img_recv,
        part_send, part_recv, mean_send, mean_recv,
    ) = rest
    diffusion, radius, obs_cells, obs_count, obs_value, obs_error = small
    members, fields, width, levels, lat, sites_max = dims
    first = observed_field + 1
    groups = ((observed_field, first), (0, observed_field), (first, fields))
    rows_each = width // n_mem
    classes = distance_classes(width)
    me = lax.axis_index("mem")
    place = lax.axis_index("space")
    right, left = lax.rem(place + 1, n_space), lax.rem(place + n_space - 1, n_space)

    load = pltpu.make_async_copy(state, st.at[:, :, 2 : 2 + width], load_sem)
    load.start()
    fetches = []
    for i, (src, dst) in enumerate(zip(small_hbm, small)):
        fetch = pltpu.make_async_copy(src, dst, small_sem.at[i])
        fetch.start()
        fetches.append(fetch)

    barrier = pltpu.get_barrier_semaphore()
    for side in (left, right):
        pl.semaphore_signal(barrier, inc=1, device_id={"space": side}, device_id_type=MESH)
    for p in range(1, n_mem):
        pl.semaphore_signal(
            barrier, inc=1, device_id={"mem": lax.rem(me + p, n_mem)}, device_id_type=MESH
        )
    pl.semaphore_wait(barrier, 2 + n_mem - 1)

    def halo(g):
        lo, hi, layers, sides = (
            (observed_field, first, 2, ((width - 2, 0), (0, width + 2))),
            (0, observed_field, 1, ((width - 1, 1), (0, width + 2))),
            (0, observed_field, 1, ((width - 2, 0), (1, width + 3))),
            (first, fields, 2, ((width - 2, 0), (0, width + 2))),
        )[g]
        copies = []
        for side, (src, dst) in enumerate(sides):
            copy = pltpu.make_async_remote_copy(
                src_ref=state.at[:, lo:hi, src : src + layers],
                dst_ref=st.at[:, lo:hi, dst : dst + layers],
                send_sem=halo_send.at[g, side],
                recv_sem=halo_recv.at[g, side],
                device_id={"space": (right, left)[side]},
                device_id_type=MESH,
            )
            copy.start()
            copies.append(copy)
        return copies

    halos = [halo(0), halo(1)]

    for fetch in fetches:
        fetch.wait()

    rates = [diffusion[f] * time_step for f in range(fields)]

    def advance(src, wind, m, row, f):
        centre = src[m, f, row]
        east, west = src[m, f, row + 1], src[m, f, row - 1]
        north = pltpu.roll(centre, lat - 1, 1)
        south = pltpu.roll(centre, 1, 1)
        spread = (east + west) + (north + south) - 4.0 * centre
        return centre + (rates[f] * spread - (wind[0] * (east - west) + wind[1] * (north - south)))

    def winds(src, m, row):
        half = 0.5 * time_step
        return src[m, 0, row] * half, src[m, 1, row] * half

    def step_one(m, x, span):
        wind = winds(st, m, x + 2)
        for f in range(*span):
            mid[m, f, x + 1] = advance(st, wind, m, x + 2, f)

    def step_two(m, x, span):
        wind = winds(mid, m, x + 1)
        for f in range(*span):
            value = advance(mid, wind, m, x + 1, f)
            adv[m, f, x] = value
            if f == observed_field:
                img[width + x, pl.ds(m, 1)] = jnp.mean(value, axis=0, keepdims=True)

    def inner(step, low, high, span):
        count = high - low

        @pl.loop(0, members * count)
        def _(i):
            step(i // count, low + i % count, span)

    def at_rows(step, rows, span):
        @pl.loop(0, members)
        def _(m):
            for x in rows:
                step(m, x, span)

    edges, inside = (0, width - 1), (1, width - 2)
    beyond = (-1, width)

    load.wait()
    inner(step_one, 1, width - 1, (0, fields))
    inner(step_two, 2, width - 2, (0, fields))

    level_at = lax.broadcasted_iota(jnp.int32, (levels, lat), 0)
    radii = jnp.ones((levels, lat), jnp.float32)
    for z in range(levels):
        radii = jnp.where(level_at == z, radius[z].astype(jnp.float32), radii)
    inverse = 1.0 / (radii * radii)
    for k, (distance, _) in enumerate(classes):
        clipped = jnp.maximum(0.0, 1.0 - float(distance) * inverse)
        table[k] = -0.5 * (clipped * clipped)

    cell_at = lax.broadcasted_iota(jnp.int32, (width, lat), 0) * lat
    cell_at = cell_at + lax.broadcasted_iota(jnp.int32, (width, lat), 1)
    count = obs_count[0]

    def precision(o):
        valid = jnp.where(o < count, 1.0, 0.0)
        error = jnp.full((width, lat), obs_error[0, o], jnp.float32)
        here = cell_at == obs_cells[0, o]
        return jnp.where(here, valid / (error * error), 0.0)

    def gather_sums(o, carry):
        weight = precision(o)
        return carry[0] + weight, carry[1] + weight * obs_value[0, o]

    zero = jnp.zeros((width, lat), jnp.float32)
    weight_sum, value_sum = lax.fori_loop(0, sites_max, gather_sums, (zero, zero), unroll=4)
    centre_value = jnp.where(
        weight_sum > 0.0, value_sum / jnp.where(weight_sum > 0.0, weight_sum, 1.0), 0.0
    )

    def gather_spread(o, carry):
        away = obs_value[0, o] - centre_value
        return carry + precision(o) * (away * away)

    obs_img[0] = weight_sum
    obs_img[1] = centre_value
    obs_img[2] = lax.fori_loop(0, sites_max, gather_spread, zero, unroll=4)

    for copy in halos[0] + halos[1]:
        copy.wait_recv()
    at_rows(step_one, edges, (0, first))
    at_rows(step_one, beyond, groups[0])
    at_rows(step_two, edges + inside, groups[0])

    for x in range(width):
        away = img[width + x] - obs_img[1, x : x + 1]
        img[width + x] = obs_img[2, x : x + 1] + obs_img[0, x : x + 1] * (away * away)

    img_copies = []
    for side, (dst, target) in enumerate(((0, right), (2 * width, left))):
        copy = pltpu.make_async_remote_copy(
            src_ref=img.at[width : 2 * width],
            dst_ref=img.at[dst : dst + width],
            send_sem=img_send.at[side],
            recv_sem=img_recv.at[side],
            device_id={"space": target},
            device_id_type=MESH,
        )
        copy.start()
        img_copies.append(copy)
    halos.append(halo(2))
    halos.append(halo(3))

    def roll_rows(low, high):
        @pl.loop(low, high)
        def _(r):
            row = img[r]
            rolled[0, r] = row
            for b in range(1, width):
                rolled[b, r] = pltpu.roll(row, b, 1) + pltpu.roll(row, lat - b, 1)

    roll_rows(width, 2 * width)
    at_rows(step_two, inside, groups[1])
    for copy in img_copies:
        copy.wait_recv()
    roll_rows(1, width)
    roll_rows(2 * width, 3 * width - 1)

    def weigh_row(x):
        for k, (_, pairs) in enumerate(classes):
            total = None
            for a, b in pairs:
                term = rolled[b, x + width - a]
                if a:
                    term = term + rolled[b, x + width + a]
                total = term if total is None else total + term
            classed[k] = total
        logs = [jnp.zeros((levels, lat), jnp.float32) for _ in range(members)]
        for k in range(len(classes)):
            taper = table[k]
            for m in range(members):
                logs[m] = logs[m] + taper * classed[k, m : m + 1]
        best = functools.reduce(jnp.maximum, logs)
        expo = [jnp.exp(value - best) for value in logs]
        total = functools.reduce(jnp.add, expo)
        part[first, x] = best + jnp.log(total)
        scale = 1.0 / total
        for m in range(members):
            gain[m, x] = expo[m] * scale

    def sum_row(x, span):
        weights = [gain[m, x] for m in range(members)]
        for f in range(*span):
            part[plane(f), x] = functools.reduce(
                jnp.add, [weights[m] * adv[m, f, x] for m in range(members)]
            )

    def plane(f):
        return f if f < first else f + 1

    spans = ((observed_field, first + 1), groups[1], (first + 1, fields + 1))

    def send_part(g, p):
        lo, hi = spans[g]
        target = lax.rem(me + p, n_mem)
        copy = pltpu.make_async_remote_copy(
            src_ref=part.at[lo:hi, pl.ds(target * rows_each, rows_each)],
            dst_ref=inbox.at[p, lo:hi],
            send_sem=part_send.at[g, p],
            recv_sem=part_recv.at[g, p],
            device_id={"mem": target},
            device_id_type=MESH,
        )
        copy.start()
        return copy

    own = me * rows_each
    part_copies = [[], [], []]
    peers = list(range(1, n_mem)) + [0]

    def spread(g, row_work):
        for p in peers:
            base = lax.rem(me + p, n_mem) * rows_each

            @pl.loop(0, rows_each)
            def _(i):
                row_work(base + i)

            if p:
                part_copies[g].append(send_part(g, p))

    def weigh_and_sum(x):
        weigh_row(x)
        sum_row(x, groups[0])

    def send_mean(g, slot, target, start, count):
        lo, hi = groups[g]
        copy = pltpu.make_async_remote_copy(
            src_ref=mean.at[lo:hi, pl.ds(start, count)],
            dst_ref=mean.at[lo:hi, pl.ds(start, count)],
            send_sem=mean_send.at[g, slot],
            recv_sem=mean_recv.at[g, slot],
            device_id={"mem": target},
            device_id_type=MESH,
        )
        copy.start()
        return copy

    square = n_mem == 4 and rows_each % 2 == 0
    relayed = (0, 1) if square else ()
    across, along = me + 1 - 2 * lax.rem(me, 2), lax.rem(me + 2, n_mem)

    def forward(g):
        if g not in relayed:
            return
        half = rows_each // 2
        mean_copies[g][0].wait_recv()
        one = send_mean(g, 3, along, across * rows_each, half)
        mean_copies[g][1].wait_recv()
        two = send_mean(g, 0, across, along * rows_each + half, half)
        forwards.extend((one, two))

    forwards = []
    mean_copies = []

    def merge(g):
        lo, hi = groups[g]
        for copy in part_copies[g]:
            copy.wait_recv()

        @pl.loop(0, rows_each)
        def _(i):
            if g == 0:
                logs = [part[first, own + i]] + [inbox[p, first, i] for p in range(1, n_mem)]
                best = functools.reduce(jnp.maximum, logs)
                expo = [jnp.exp(value - best) for value in logs]
                scale = 1.0 / functools.reduce(jnp.add, expo)
                weights = [value * scale for value in expo]
                for p in range(n_mem):
                    share[p, i] = weights[p]
            else:
                weights = [share[p, i] for p in range(n_mem)]
            for f in range(lo, hi):
                total = weights[0] * part[plane(f), own + i]
                for p in range(1, n_mem):
                    total = total + weights[p] * inbox[p, plane(f), i]
                mean[f, own + i] = total

        if g in relayed:
            routes = ((1, across), (2, along))
        else:
            routes = [(p, lax.rem(me + p, n_mem)) for p in range(1, n_mem)]
        mean_copies.append([send_mean(g, p, to, own, rows_each) for p, to in routes])

    spread(0, weigh_and_sum)
    for copy in halos[2]:
        copy.wait_recv()
    at_rows(step_one, beyond, groups[1])
    at_rows(step_two, edges, groups[1])
    spread(1, lambda x: sum_row(x, groups[1]))
    merge(0)
    for copy in halos[3]:
        copy.wait_recv()
    at_rows(step_one, beyond + edges, groups[2])
    at_rows(step_two, edges + inside, groups[2])
    spread(2, lambda x: sum_row(x, groups[2]))
    merge(1)
    forward(0)
    merge(2)
    forward(1)

    for g, copies in enumerate(mean_copies):
        for copy in copies:
            if g not in relayed:
                copy.wait_recv()
    for copy in forwards:
        copy.wait_recv()
    for copy in sum(halos, []) + img_copies + forwards:
        copy.wait_send()
    for g in range(3):
        for copy in part_copies[g] + mean_copies[g]:
            copy.wait_send()


def local(n_mem, n_space, state, diffusion, radius, obs_cells, obs_count, obs_value, obs_error):
    members, fields, width, levels, lat = state.shape
    sites_max = obs_cells.shape[1]
    dims = (members, fields, width, levels, lat, sites_max)
    rows_each = width // n_mem
    n_class = len(distance_classes(width))
    dma = pltpu.SemaphoreType.DMA

    def vmem(*shape):
        return pltpu.VMEM(shape, jnp.float32)

    small = (diffusion, radius, obs_cells, obs_count, obs_value, obs_error)
    hbm = pl.BlockSpec(memory_space=pltpu.HBM)
    adv, mean = pl.pallas_call(
        functools.partial(kernel, n_mem, n_space, dims),
        out_shape=[
            pltpu.VMEM(state.shape, jnp.float32),
            pltpu.VMEM(state.shape[1:], jnp.float32),
        ],
        in_specs=[hbm] * 7,
        out_specs=[pl.BlockSpec(memory_space=pltpu.VMEM)] * 2,
        scratch_shapes=[pltpu.SMEM(value.shape, value.dtype) for value in small]
        + [
            vmem(members, fields, width + 4, levels, lat),
            vmem(members, fields, width + 2, levels, lat),
            vmem(3, width, lat),
            vmem(3 * width, members, lat),
            vmem(width, 3 * width, members, lat),
            vmem(n_class, levels, lat),
            vmem(n_class, members, lat),
            vmem(members, width, levels, lat),
            vmem(1 + fields, width, levels, lat),
            vmem(n_mem, 1 + fields, rows_each, levels, lat),
            vmem(n_mem, rows_each, levels, lat),
            dma((len(small),)),
            dma,
            dma((4, 2)),
            dma((4, 2)),
            dma((2,)),
            dma((2,)),
            dma((3, n_mem)),
            dma((3, n_mem)),
            dma((3, n_mem)),
            dma((3, n_mem)),
        ],
        compiler_params=pltpu.CompilerParams(
            collective_id=0, has_side_effects=True, vmem_limit_bytes=24 * 2**20
        ),
    )(*[value if value.size == 1 else pltpu.with_memory_space_constraint(value, pltpu.HBM) for value in (state, *small)])
    return adv + blend_share * (mean[None] - adv)


def solution(mesh):
    return jax.shard_map(
        functools.partial(local, mesh.shape["mem"], mesh.shape["space"]),
        mesh=mesh,
        in_specs=(
            P("mem", None, "space", None, None),
            P(),
            P(),
            P("space", None),
            P("space"),
            P("space", None),
            P("space", None),
        ),
        out_specs=P("mem", None, "space", None, None),
        check_vma=False,
    )
```

```python
import functools
import math

import jax
import jax.numpy as jnp
from jax import lax
from jax.experimental import pallas as pl
from jax.experimental.pallas import tpu as pltpu
from jax.sharding import PartitionSpec as P

time_step = 0.2
blend_share = 0.5
observed_field = 2
MESH = pl.DeviceIdType.MESH


def distance_classes(reach):
    classes = {}
    for a in range(reach):
        for b in range(reach):
            if a * a + b * b < reach * reach:
                classes.setdefault(a * a + b * b, []).append((a, b))
    return sorted(classes.items())


def kernel(
    n_mem, n_space, dims,
    state, *rest,
):
    small_hbm, rest = rest[:6], rest[6:]
    adv, mean = rest[:2]
    small, rest = rest[2:8], rest[8:]
    (
        st, mid, obs_img, img, rolled, table, classed, gain, part, inbox, share,
        small_sem, load_sem, halo_send, halo_recv, img_send, img_recv,
        part_send, part_recv, mean_send, mean_recv,
    ) = rest
    diffusion, radius, obs_cells, obs_count, obs_value, obs_error = small
    members, fields, width, levels, lat, sites_max = dims
    first = observed_field + 1
    groups = ((observed_field, first), (0, observed_field), (first, fields))
    rows_each = width // n_mem
    classes = distance_classes(width)
    me = lax.axis_index("mem")
    place = lax.axis_index("space")
    right, left = lax.rem(place + 1, n_space), lax.rem(place + n_space - 1, n_space)

    load = pltpu.make_async_copy(state, st.at[:, :, 2 : 2 + width], load_sem)
    load.start()
    fetches = []
    for i, (src, dst) in enumerate(zip(small_hbm, small)):
        fetch = pltpu.make_async_copy(src, dst, small_sem.at[i])
        fetch.start()
        fetches.append(fetch)

    barrier = pltpu.get_barrier_semaphore()
    for side in (left, right):
        pl.semaphore_signal(barrier, inc=1, device_id={"space": side}, device_id_type=MESH)
    for p in range(1, n_mem):
        pl.semaphore_signal(
            barrier, inc=1, device_id={"mem": lax.rem(me + p, n_mem)}, device_id_type=MESH
        )
    pl.semaphore_wait(barrier, 2 + n_mem - 1)

    def halo(g):
        lo, hi, layers, sides = (
            (observed_field, first, 2, ((width - 2, 0), (0, width + 2))),
            (0, observed_field, 1, ((width - 1, 1), (0, width + 2))),
            (0, observed_field, 1, ((width - 2, 0), (1, width + 3))),
            (first, fields, 2, ((width - 2, 0), (0, width + 2))),
        )[g]
        copies = []
        for side, (src, dst) in enumerate(sides):
            copy = pltpu.make_async_remote_copy(
                src_ref=state.at[:, lo:hi, src : src + layers],
                dst_ref=st.at[:, lo:hi, dst : dst + layers],
                send_sem=halo_send.at[g, side],
                recv_sem=halo_recv.at[g, side],
                device_id={"space": (right, left)[side]},
                device_id_type=MESH,
            )
            copy.start()
            copies.append(copy)
        return copies

    halos = [halo(0), halo(1)]

    for fetch in fetches:
        fetch.wait()

    rates = [diffusion[f] * time_step for f in range(fields)]

    def advance(src, wind, m, row, f):
        centre = src[m, f, row]
        east, west = src[m, f, row + 1], src[m, f, row - 1]
        north = pltpu.roll(centre, lat - 1, 1)
        south = pltpu.roll(centre, 1, 1)
        spread = (east + west) + (north + south) - 4.0 * centre
        return centre + (rates[f] * spread - (wind[0] * (east - west) + wind[1] * (north - south)))

    def winds(src, m, row):
        half = 0.5 * time_step
        return src[m, 0, row] * half, src[m, 1, row] * half

    def step_one(m, x, span):
        wind = winds(st, m, x + 2)
        for f in range(*span):
            mid[m, f, x + 1] = advance(st, wind, m, x + 2, f)

    def step_two(m, x, span):
        wind = winds(mid, m, x + 1)
        for f in range(*span):
            value = advance(mid, wind, m, x + 1, f)
            adv[m, f, x] = value
            if f == observed_field:
                img[width + x, pl.ds(m, 1)] = jnp.mean(value, axis=0, keepdims=True)

    def inner(step, low, high, span):
        count = high - low

        @pl.loop(0, members * count, unroll=math.gcd(members * count, 8))
        def _(i):
            step(i // count, low + i % count, span)

    def at_rows(step, rows, span):
        @pl.loop(0, members, unroll=members)
        def _(m):
            for x in rows:
                step(m, x, span)

    edges, inside = (0, width - 1), (1, width - 2)
    beyond = (-1, width)

    load.wait()
    inner(step_one, 1, width - 1, (0, fields))
    inner(step_two, 2, width - 2, (0, fields))

    level_at = lax.broadcasted_iota(jnp.int32, (levels, lat), 0)
    radii = jnp.ones((levels, lat), jnp.float32)
    for z in range(levels):
        radii = jnp.where(level_at == z, radius[z].astype(jnp.float32), radii)
    inverse = 1.0 / (radii * radii)
    for k, (distance, _) in enumerate(classes):
        clipped = jnp.maximum(0.0, 1.0 - float(distance) * inverse)
        table[k] = -0.5 * (clipped * clipped)

    cell_at = lax.broadcasted_iota(jnp.int32, (width, lat), 0) * lat
    cell_at = cell_at + lax.broadcasted_iota(jnp.int32, (width, lat), 1)
    count = obs_count[0]

    def precision(o):
        valid = jnp.where(o < count, 1.0, 0.0)
        error = jnp.full((width, lat), obs_error[0, o], jnp.float32)
        here = cell_at == obs_cells[0, o]
        return jnp.where(here, valid / (error * error), 0.0)

    def gather_sums(o, carry):
        weight = precision(o)
        return carry[0] + weight, carry[1] + weight * obs_value[0, o]

    zero = jnp.zeros((width, lat), jnp.float32)
    weight_sum, value_sum = lax.fori_loop(0, sites_max, gather_sums, (zero, zero), unroll=4)
    centre_value = jnp.where(
        weight_sum > 0.0, value_sum / jnp.where(weight_sum > 0.0, weight_sum, 1.0), 0.0
    )

    def gather_spread(o, carry):
        away = obs_value[0, o] - centre_value
        return carry + precision(o) * (away * away)

    obs_img[0] = weight_sum
    obs_img[1] = centre_value
    obs_img[2] = lax.fori_loop(0, sites_max, gather_spread, zero, unroll=4)

    for copy in halos[0] + halos[1]:
        copy.wait_recv()
    at_rows(step_one, edges, (0, first))
    at_rows(step_one, beyond, groups[0])
    at_rows(step_two, edges + inside, groups[0])

    for x in range(width):
        away = img[width + x] - obs_img[1, x : x + 1]
        img[width + x] = obs_img[2, x : x + 1] + obs_img[0, x : x + 1] * (away * away)

    img_copies = []
    for side, (dst, target) in enumerate(((0, right), (2 * width, left))):
        copy = pltpu.make_async_remote_copy(
            src_ref=img.at[width : 2 * width],
            dst_ref=img.at[dst : dst + width],
            send_sem=img_send.at[side],
            recv_sem=img_recv.at[side],
            device_id={"space": target},
            device_id_type=MESH,
        )
        copy.start()
        img_copies.append(copy)
    halos.append(halo(2))
    halos.append(halo(3))

    def roll_rows(low, high):
        @pl.loop(low, high)
        def _(r):
            row = img[r]
            rolled[0, r] = row
            for b in range(1, width):
                rolled[b, r] = pltpu.roll(row, b, 1) + pltpu.roll(row, lat - b, 1)

    roll_rows(width, 2 * width)
    at_rows(step_two, inside, groups[1])
    for copy in img_copies:
        copy.wait_recv()
    roll_rows(1, width)
    roll_rows(2 * width, 3 * width - 1)

    def weigh_row(x):
        for k, (_, pairs) in enumerate(classes):
            total = None
            for a, b in pairs:
                term = rolled[b, x + width - a]
                if a:
                    term = term + rolled[b, x + width + a]
                total = term if total is None else total + term
            classed[k] = total
        logs = [jnp.zeros((levels, lat), jnp.float32) for _ in range(members)]
        for k in range(len(classes)):
            taper = table[k]
            for m in range(members):
                logs[m] = logs[m] + taper * classed[k, m : m + 1]
        best = functools.reduce(jnp.maximum, logs)
        expo = [jnp.exp(value - best) for value in logs]
        total = functools.reduce(jnp.add, expo)
        part[first, x] = best + jnp.log(total)
        scale = 1.0 / total
        for m in range(members):
            gain[m, x] = expo[m] * scale

    def sum_row(x, span):
        weights = [gain[m, x] for m in range(members)]
        for f in range(*span):
            part[plane(f), x] = functools.reduce(
                jnp.add, [weights[m] * adv[m, f, x] for m in range(members)]
            )

    def plane(f):
        return f if f < first else f + 1

    spans = ((observed_field, first + 1), groups[1], (first + 1, fields + 1))

    def send_part(g, p):
        lo, hi = spans[g]
        target = lax.rem(me + p, n_mem)
        copy = pltpu.make_async_remote_copy(
            src_ref=part.at[lo:hi, pl.ds(target * rows_each, rows_each)],
            dst_ref=inbox.at[p, lo:hi],
            send_sem=part_send.at[g, p],
            recv_sem=part_recv.at[g, p],
            device_id={"mem": target},
            device_id_type=MESH,
        )
        copy.start()
        return copy

    own = me * rows_each
    part_copies = [[], [], []]
    peers = list(range(1, n_mem)) + [0]

    def spread(g, row_work):
        for p in peers:
            base = lax.rem(me + p, n_mem) * rows_each

            @pl.loop(0, rows_each)
            def _(i):
                row_work(base + i)

            if p:
                part_copies[g].append(send_part(g, p))

    def weigh_and_sum(x):
        weigh_row(x)
        sum_row(x, groups[0])

    def send_mean(g, slot, target, start, count):
        lo, hi = groups[g]
        copy = pltpu.make_async_remote_copy(
            src_ref=mean.at[lo:hi, pl.ds(start, count)],
            dst_ref=mean.at[lo:hi, pl.ds(start, count)],
            send_sem=mean_send.at[g, slot],
            recv_sem=mean_recv.at[g, slot],
            device_id={"mem": target},
            device_id_type=MESH,
        )
        copy.start()
        return copy

    square = n_mem == 4 and rows_each % 2 == 0
    relayed = (0, 1) if square else ()
    across, along = me + 1 - 2 * lax.rem(me, 2), lax.rem(me + 2, n_mem)

    def forward(g):
        if g not in relayed:
            return
        half = rows_each // 2
        mean_copies[g][0].wait_recv()
        one = send_mean(g, 3, along, across * rows_each, half)
        mean_copies[g][1].wait_recv()
        two = send_mean(g, 0, across, along * rows_each + half, half)
        forwards.extend((one, two))

    forwards = []
    mean_copies = []

    def merge(g):
        lo, hi = groups[g]
        for copy in part_copies[g]:
            copy.wait_recv()

        @pl.loop(0, rows_each)
        def _(i):
            if g == 0:
                logs = [part[first, own + i]] + [inbox[p, first, i] for p in range(1, n_mem)]
                best = functools.reduce(jnp.maximum, logs)
                expo = [jnp.exp(value - best) for value in logs]
                scale = 1.0 / functools.reduce(jnp.add, expo)
                weights = [value * scale for value in expo]
                for p in range(n_mem):
                    share[p, i] = weights[p]
            else:
                weights = [share[p, i] for p in range(n_mem)]
            for f in range(lo, hi):
                total = weights[0] * part[plane(f), own + i]
                for p in range(1, n_mem):
                    total = total + weights[p] * inbox[p, plane(f), i]
                mean[f, own + i] = total

        if g in relayed:
            routes = ((1, across), (2, along))
        else:
            routes = [(p, lax.rem(me + p, n_mem)) for p in range(1, n_mem)]
        mean_copies.append([send_mean(g, p, to, own, rows_each) for p, to in routes])

    spread(0, weigh_and_sum)
    for copy in halos[2]:
        copy.wait_recv()
    at_rows(step_one, beyond, groups[1])
    at_rows(step_two, edges, groups[1])
    spread(1, lambda x: sum_row(x, groups[1]))
    merge(0)
    for copy in halos[3]:
        copy.wait_recv()
    at_rows(step_one, beyond + edges, groups[2])
    at_rows(step_two, edges + inside, groups[2])
    spread(2, lambda x: sum_row(x, groups[2]))
    merge(1)
    forward(0)
    merge(2)
    forward(1)

    for g, copies in enumerate(mean_copies):
        for copy in copies:
            if g not in relayed:
                copy.wait_recv()
    for copy in forwards:
        copy.wait_recv()
    for copy in sum(halos, []) + img_copies + forwards:
        copy.wait_send()
    for g in range(3):
        for copy in part_copies[g] + mean_copies[g]:
            copy.wait_send()


def local(n_mem, n_space, state, diffusion, radius, obs_cells, obs_count, obs_value, obs_error):
    members, fields, width, levels, lat = state.shape
    sites_max = obs_cells.shape[1]
    dims = (members, fields, width, levels, lat, sites_max)
    rows_each = width // n_mem
    n_class = len(distance_classes(width))
    dma = pltpu.SemaphoreType.DMA

    def vmem(*shape):
        return pltpu.VMEM(shape, jnp.float32)

    small = (diffusion, radius, obs_cells, obs_count, obs_value, obs_error)
    hbm = pl.BlockSpec(memory_space=pltpu.HBM)
    adv, mean = pl.pallas_call(
        functools.partial(kernel, n_mem, n_space, dims),
        out_shape=[
            pltpu.VMEM(state.shape, jnp.float32),
            pltpu.VMEM(state.shape[1:], jnp.float32),
        ],
        in_specs=[hbm] * 7,
        out_specs=[pl.BlockSpec(memory_space=pltpu.VMEM)] * 2,
        scratch_shapes=[pltpu.SMEM(value.shape, value.dtype) for value in small]
        + [
            vmem(members, fields, width + 4, levels, lat),
            vmem(members, fields, width + 2, levels, lat),
            vmem(3, width, lat),
            vmem(3 * width, members, lat),
            vmem(width, 3 * width, members, lat),
            vmem(n_class, levels, lat),
            vmem(n_class, members, lat),
            vmem(members, width, levels, lat),
            vmem(1 + fields, width, levels, lat),
            vmem(n_mem, 1 + fields, rows_each, levels, lat),
            vmem(n_mem, rows_each, levels, lat),
            dma((len(small),)),
            dma,
            dma((4, 2)),
            dma((4, 2)),
            dma((2,)),
            dma((2,)),
            dma((3, n_mem)),
            dma((3, n_mem)),
            dma((3, n_mem)),
            dma((3, n_mem)),
        ],
        compiler_params=pltpu.CompilerParams(
            collective_id=0, has_side_effects=True, vmem_limit_bytes=24 * 2**20
        ),
    )(*[value if value.size == 1 else pltpu.with_memory_space_constraint(value, pltpu.HBM) for value in (state, *small)])
    return adv + blend_share * (mean[None] - adv)


def solution(mesh):
    return jax.shard_map(
        functools.partial(local, mesh.shape["mem"], mesh.shape["space"]),
        mesh=mesh,
        in_specs=(
            P("mem", None, "space", None, None),
            P(),
            P(),
            P("space", None),
            P("space"),
            P("space", None),
            P("space", None),
        ),
        out_specs=P("mem", None, "space", None, None),
        check_vma=False,
    )
```

```python
import functools
import math

import jax
import jax.numpy as jnp
from jax import lax
from jax.experimental import pallas as pl
from jax.experimental.pallas import tpu as pltpu
from jax.sharding import PartitionSpec as P

time_step = 0.2
blend_share = 0.5
observed_field = 2
lanes, sublanes = 128, 8
MESH = pl.DeviceIdType.MESH


def distance_classes(reach):
    classes = {}
    for a in range(reach):
        for b in range(reach):
            if a * a + b * b < reach * reach:
                classes.setdefault(a * a + b * b, []).append((a, b))
    return sorted(classes.items())


def radius_range(width):
    return range(width // 2, width + 1)


def row_of(owner, j, n_mem, width):
    each = width // n_mem
    if each != 2:
        return owner * each + j
    half = n_mem // 2
    return half + owner if j else owner + (owner // half) * (width - n_mem)


def kernel(
    n_mem, n_space, dims,
    state, *rest,
):
    small_hbm, rest = rest[:6], rest[6:]
    adv, mean = rest[:2]
    small, rest = rest[2:8], rest[8:]
    (
        st, mid, obs_img, img, rolled, gain_class, gain, part, inbox, logs_out, logs_in, share_class, share,
        small_sem, load_sem, halo_send, halo_recv, img_send, img_recv,
        part_send, part_recv, log_send, log_recv, mean_send, mean_recv,
    ) = rest
    diffusion, radius, obs_cells, obs_count, obs_value, obs_error = small
    members, fields, width, levels, lat, sites_max = dims
    first = observed_field + 1
    groups = ((observed_field, first), (0, observed_field), (first, fields))
    each = width // n_mem
    chunks = lat // lanes
    radii = radius_range(width)
    classes = distance_classes(width)
    me = lax.axis_index("mem")
    place = lax.axis_index("space")
    right, left = lax.rem(place + 1, n_space), lax.rem(place + n_space - 1, n_space)

    barrier = pltpu.get_barrier_semaphore()
    for side in (left, right):
        pl.semaphore_signal(barrier, inc=1, device_id={"space": side}, device_id_type=MESH)
    for p in range(1, n_mem):
        pl.semaphore_signal(
            barrier, inc=1, device_id={"mem": lax.rem(me + p, n_mem)}, device_id_type=MESH
        )

    load = pltpu.make_async_copy(state, st.at[:, :, 2 : 2 + width], load_sem)
    load.start()
    fetches = []
    for i, (src, dst) in enumerate(zip(small_hbm, small)):
        fetch = pltpu.make_async_copy(src, dst, small_sem.at[i])
        fetch.start()
        fetches.append(fetch)

    pl.semaphore_wait(barrier, 2 + n_mem - 1)

    def halo(g):
        lo, hi, layers, sides = (
            (observed_field, first, 2, ((width - 2, 0), (0, width + 2))),
            (0, observed_field, 1, ((width - 1, 1), (0, width + 2))),
            (0, observed_field, 1, ((width - 2, 0), (1, width + 3))),
            (first, fields, 2, ((width - 2, 0), (0, width + 2))),
        )[g]
        copies = []
        for side, (src, dst) in enumerate(sides):
            copy = pltpu.make_async_remote_copy(
                src_ref=state.at[:, lo:hi, src : src + layers],
                dst_ref=st.at[:, lo:hi, dst : dst + layers],
                send_sem=halo_send.at[g, side],
                recv_sem=halo_recv.at[g, side],
                device_id={"space": (right, left)[side]},
                device_id_type=MESH,
            )
            copy.start()
            copies.append(copy)
        return copies

    halos = [halo(0), halo(1)]

    for fetch in fetches:
        fetch.wait()

    rates = [diffusion[f] * time_step for f in range(fields)]

    def advance(src, wind, m, row, f):
        centre = src[m, f, row]
        east, west = src[m, f, row + 1], src[m, f, row - 1]
        north = pltpu.roll(centre, lat - 1, 1)
        south = pltpu.roll(centre, 1, 1)
        spread = (east + west) + (north + south) - 4.0 * centre
        return centre + (rates[f] * spread - (wind[0] * (east - west) + wind[1] * (north - south)))

    def winds(src, m, row):
        half = 0.5 * time_step
        return src[m, 0, row] * half, src[m, 1, row] * half

    def step_one(m, x, span):
        wind = winds(st, m, x + 2)
        for f in range(*span):
            mid[m, f, x + 1] = advance(st, wind, m, x + 2, f)

    def step_two(m, x, span):
        wind = winds(mid, m, x + 1)
        for f in range(*span):
            value = advance(mid, wind, m, x + 1, f)
            adv[m, f, x] = value
            if f == observed_field:
                column = jnp.mean(value, axis=0, keepdims=True)
                for h in range(chunks):
                    img[m, h, pl.ds(width + x, 1)] = column[:, h * lanes : (h + 1) * lanes]

    def inner(step, low, high, span):
        count = high - low

        @pl.loop(0, members * count, unroll=math.gcd(members * count, 8))
        def _(i):
            step(i // count, low + i % count, span)

    def at_rows(step, rows, span):
        @pl.loop(0, members, unroll=members)
        def _(m):
            for x in rows:
                step(m, x, span)

    edges, inside = (0, width - 1), (1, width - 2)
    beyond = (-1, width)

    load.wait()
    inner(step_one, 1, width - 1, (0, fields))
    inner(step_two, 2, width - 2, (0, fields))

    cell_at = lax.broadcasted_iota(jnp.int32, (width, lat), 0) * lat
    cell_at = cell_at + lax.broadcasted_iota(jnp.int32, (width, lat), 1)
    count = obs_count[0]

    def precision(o):
        valid = jnp.where(o < count, 1.0, 0.0)
        error = jnp.full((width, lat), obs_error[0, o], jnp.float32)
        here = cell_at == obs_cells[0, o]
        return jnp.where(here, valid / (error * error), 0.0)

    def gather_sums(o, carry):
        weight = precision(o)
        return carry[0] + weight, carry[1] + weight * obs_value[0, o]

    zero = jnp.zeros((width, lat), jnp.float32)
    weight_sum, value_sum = lax.fori_loop(0, sites_max, gather_sums, (zero, zero), unroll=4)
    centre_value = jnp.where(
        weight_sum > 0.0, value_sum / jnp.where(weight_sum > 0.0, weight_sum, 1.0), 0.0
    )

    def gather_spread(o, carry):
        away = obs_value[0, o] - centre_value
        return carry + precision(o) * (away * away)

    obs_img[0] = weight_sum
    obs_img[1] = centre_value
    obs_img[2] = lax.fori_loop(0, sites_max, gather_spread, zero, unroll=4)

    level_at = lax.broadcasted_iota(jnp.int32, (levels, lanes), 0)
    level_radius = jnp.zeros((levels, lanes), jnp.int32)
    for z in range(levels):
        level_radius = jnp.where(level_at == z, radius[z], level_radius)
    logs_out[...] = jnp.zeros_like(logs_out)

    for copy in halos[0] + halos[1]:
        copy.wait_recv()
    at_rows(step_one, edges, (0, first))
    at_rows(step_one, beyond, groups[0])
    at_rows(step_two, edges + inside, groups[0])

    own_rows = pl.ds(width, width)
    for m in range(members):
        for h in range(chunks):
            part_lanes = slice(h * lanes, (h + 1) * lanes)
            away = img[m, h, own_rows] - obs_img[1, :, part_lanes]
            img[m, h, own_rows] = obs_img[2, :, part_lanes] + obs_img[0, :, part_lanes] * (away * away)

    img_copies = []
    for side, (dst, target) in enumerate(((0, right), (2 * width, left))):
        copy = pltpu.make_async_remote_copy(
            src_ref=img.at[:, :, width : 2 * width],
            dst_ref=img.at[:, :, dst : dst + width],
            send_sem=img_send.at[side],
            recv_sem=img_recv.at[side],
            device_id={"space": target},
            device_id_type=MESH,
        )
        copy.start()
        img_copies.append(copy)
    halos.append(halo(2))
    halos.append(halo(3))

    def roll_rows(tile):
        rows = pl.ds(tile * width, width)

        @pl.loop(0, members, unroll=members)
        def _(m):
            row = jnp.concatenate([img[m, h, rows] for h in range(chunks)], axis=1)
            for b in range(1, width):
                both = pltpu.roll(row, b, 1) + pltpu.roll(row, lat - b, 1)
                for h in range(chunks):
                    rolled[b - 1, m, h, rows] = both[:, h * lanes : (h + 1) * lanes]

    roll_rows(1)
    at_rows(step_two, inside, groups[1])
    for copy in img_copies:
        copy.wait_recv()
    roll_rows(0)
    roll_rows(2)

    def shifted(m, h, a, b):
        source = img.at[m, h] if b == 0 else rolled.at[b - 1, m, h]
        term = source[pl.ds(width - a, width)]
        return term + source[pl.ds(width + a, width)] if a else term

    @pl.loop(0, chunks)
    def _(h):
        logs = []
        for m in range(members):
            sums = [None] * len(radii)
            for distance, pairs in classes:
                total = functools.reduce(jnp.add, [shifted(m, h, a, b) for a, b in pairs])
                for i, reach in enumerate(radii):
                    if distance < reach * reach:
                        taper = 1.0 - distance / (reach * reach)
                        term = (-0.5 * taper * taper) * total
                        sums[i] = term if sums[i] is None else sums[i] + term
            logs.append(sums)
        for i in range(len(radii)):
            best = functools.reduce(jnp.maximum, [logs[m][i] for m in range(members)])
            expo = [jnp.exp(logs[m][i] - best) for m in range(members)]
            total = functools.reduce(jnp.add, expo)
            scale = 1.0 / total
            for m in range(members):
                gain_class[m, i, h] = expo[m] * scale
            local_log = best + jnp.log(total)
            for owner in range(n_mem):
                for j in range(each):
                    x = row_of(owner, j, n_mem, width)
                    logs_out[owner, j, h, pl.ds(i, 1)] = local_log[x : x + 1]

    def expand(read):
        parts = []
        for h in range(chunks):
            value = jnp.broadcast_to(read(0, h), (levels, lanes))
            for i in range(1, len(radii)):
                value = jnp.where(level_radius == radii[i], read(i, h), value)
            parts.append(value)
        return jnp.concatenate(parts, axis=1)

    order = [observed_field] + [f for f in range(fields) if f != observed_field]
    late = 1 if each == 2 else each
    units = [
        ((0, 1), (0, each)),
        ((1, fields), (late, each)),
        ((1, first), (0, late)),
        ((first, fields), (0, late)),
    ]

    def sum_row(u, owner, j):
        x = row_of(owner, j, n_mem, width)
        if u == 0:
            for m in range(members):
                gain[m, x] = expand(lambda i, h: gain_class[m, i, h, pl.ds(x, 1)])
        weights = [gain[m, x] for m in range(members)]
        for k in range(*units[u][0]):
            part[owner, k, j] = functools.reduce(
                jnp.add, [weights[m] * adv[m, order[k], x] for m in range(members)]
            )

    def send(src, dst, send_sem, recv_sem, target):
        copy = pltpu.make_async_remote_copy(
            src_ref=src, dst_ref=dst, send_sem=send_sem, recv_sem=recv_sem,
            device_id={"mem": target}, device_id_type=MESH,
        )
        copy.start()
        return copy

    part_copies = [[] for _ in units]
    peers = list(range(1, n_mem)) + [0]

    def spread(u):
        (lo, hi), (low, high) = units[u]
        if low == high:
            return
        for p in peers:
            owner = lax.rem(me + p, n_mem)
            if u == 0 and p:
                part_copies[u].append(
                    send(logs_out.at[owner], logs_in.at[p], log_send.at[p], log_recv.at[p], owner)
                )
            for j in range(low, high):
                sum_row(u, owner, j)
            if p:
                box = (slice(lo, hi), slice(low, high))
                part_copies[u].append(
                    send(
                        part.at[(owner,) + box], inbox.at[(p,) + box],
                        part_send.at[u, p], part_recv.at[u, p], owner,
                    )
                )

    pieces = [[(0, j, j) for j in range(each)]]
    pieces.append([(g, j, each + 2 * (j - late) + g - 1) for j in range(late, each) for g in (1, 2)])
    pieces.append([(1, j, 3 * each - 2 * late + j) for j in range(late)])
    pieces.append([(2, j, 3 * each - late + j) for j in range(late)])
    mean_copies = []

    def send_mean(piece, p):
        g, j, n = piece
        lo, hi = groups[g]
        block = mean.at[lo:hi, pl.ds(row_of(me, j, n_mem, width), 1)]
        return send(block, block, mean_send.at[n, p], mean_recv.at[n, p], lax.rem(me + p, n_mem))

    def merge(u):
        (lo, hi), (low, high) = units[u]
        if low == high:
            return
        for copy in part_copies[u]:
            copy.wait_recv()
        for j in range(low, high):
            if u == 0:
                logs = [logs_out[me, j]] + [logs_in[p, j] for p in range(1, n_mem)]
                best = functools.reduce(jnp.maximum, logs)
                expo = [jnp.exp(value - best) for value in logs]
                scale = 1.0 / functools.reduce(jnp.add, expo)
                for p in range(n_mem):
                    share_class[p, j] = expo[p] * scale
                for p in range(n_mem):
                    share[p, j] = expand(lambda i, h: share_class[p, j, h, pl.ds(i, 1)])
            weights = [share[p, j] for p in range(n_mem)]
            for k in range(lo, hi):
                total = weights[0] * part[me, k, j]
                for p in range(1, n_mem):
                    total = total + weights[p] * inbox[p, k, j]
                mean[order[k], row_of(me, j, n_mem, width)] = total
        for piece in pieces[u]:
            for p in range(1, n_mem):
                mean_copies.append(send_mean(piece, p))

    def late_winds():
        for copy in halos[2]:
            copy.wait_recv()
        at_rows(step_one, beyond, groups[1])
        at_rows(step_two, edges, groups[1])
        spread(2)

    def late_rest():
        for copy in halos[3]:
            copy.wait_recv()
        at_rows(step_one, beyond + edges, groups[2])
        at_rows(step_two, edges + inside, groups[2])
        spread(3)

    spread(0)
    spread(1)
    late_winds()
    merge(0)
    late_rest()
    merge(1)
    merge(2)
    merge(3)

    for copy in mean_copies:
        copy.wait_recv()
    for copy in sum(halos, []) + img_copies + sum(part_copies, []) + mean_copies:
        copy.wait_send()


def local(n_mem, n_space, state, diffusion, radius, obs_cells, obs_count, obs_value, obs_error):
    members, fields, width, levels, lat = state.shape
    sites_max = obs_cells.shape[1]
    dims = (members, fields, width, levels, lat, sites_max)
    each = width // n_mem
    chunks = lat // lanes
    n_radii = len(radius_range(width))
    slots = -(-n_radii // sublanes) * sublanes
    n_pieces = 3 * each
    dma = pltpu.SemaphoreType.DMA

    def vmem(*shape):
        return pltpu.VMEM(shape, jnp.float32)

    small = (diffusion, radius, obs_cells, obs_count, obs_value, obs_error)
    held = [
        value if value.size == 1 else pltpu.with_memory_space_constraint(value, pltpu.HBM)
        for value in (state, *small)
    ]
    hbm = pl.BlockSpec(memory_space=pltpu.HBM)
    adv, mean = pl.pallas_call(
        functools.partial(kernel, n_mem, n_space, dims),
        out_shape=[
            pltpu.VMEM(state.shape, jnp.float32),
            pltpu.VMEM(state.shape[1:], jnp.float32),
        ],
        in_specs=[hbm] * 7,
        out_specs=[pl.BlockSpec(memory_space=pltpu.VMEM)] * 2,
        scratch_shapes=[pltpu.SMEM(value.shape, value.dtype) for value in small]
        + [
            vmem(members, fields, width + 4, levels, lat),
            vmem(members, fields, width + 2, levels, lat),
            vmem(3, width, lat),
            vmem(members, chunks, 3 * width, lanes),
            vmem(width - 1, members, chunks, 3 * width, lanes),
            vmem(members, n_radii, chunks, width, lanes),
            vmem(members, width, levels, lat),
            vmem(n_mem, fields, each, levels, lat),
            vmem(n_mem, fields, each, levels, lat),
            vmem(n_mem, each, chunks, slots, lanes),
            vmem(n_mem, each, chunks, slots, lanes),
            vmem(n_mem, each, chunks, slots, lanes),
            vmem(n_mem, each, levels, lat),
            dma((len(small),)),
            dma,
            dma((4, 2)),
            dma((4, 2)),
            dma((2,)),
            dma((2,)),
            dma((4, n_mem)),
            dma((4, n_mem)),
            dma((n_mem,)),
            dma((n_mem,)),
            dma((n_pieces, n_mem)),
            dma((n_pieces, n_mem)),
        ],
        compiler_params=pltpu.CompilerParams(
            collective_id=0, has_side_effects=True, vmem_limit_bytes=24 * 2**20
        ),
    )(*held)
    return adv + blend_share * (mean[None] - adv)


def solution(mesh):
    return jax.shard_map(
        functools.partial(local, mesh.shape["mem"], mesh.shape["space"]),
        mesh=mesh,
        in_specs=(
            P("mem", None, "space", None, None),
            P(),
            P(),
            P("space", None),
            P("space"),
            P("space", None),
            P("space", None),
        ),
        out_specs=P("mem", None, "space", None, None),
        check_vma=False,
    )
```

```python
import functools
import math

import jax
import jax.numpy as jnp
from jax import lax
from jax.experimental import pallas as pl
from jax.experimental.pallas import tpu as pltpu
from jax.sharding import PartitionSpec as P

time_step = 0.2
blend_share = 0.5
observed_field = 2
lanes, sublanes = 128, 8
MESH = pl.DeviceIdType.MESH


def distance_classes(reach):
    classes = {}
    for a in range(reach):
        for b in range(reach):
            if a * a + b * b < reach * reach:
                classes.setdefault(a * a + b * b, []).append((a, b))
    return sorted(classes.items())


def radius_range(width):
    return range(width // 2, width + 1)


def row_of(owner, j, n_mem, width):
    each = width // n_mem
    if each != 2:
        return owner * each + j
    half = n_mem // 2
    return half + owner if j else owner + (owner // half) * (width - n_mem)


def kernel(
    n_mem, n_space, dims,
    state, *rest,
):
    small_hbm, rest = rest[:6], rest[6:]
    adv, mean = rest[:2]
    small, rest = rest[2:8], rest[8:]
    (
        st, mid, obs_img, img, rolled, gain_class, gain, part, inbox, logs_out, logs_in, share_class, share,
        small_sem, load_sem, halo_send, halo_recv, img_send, img_recv,
        part_send, part_recv, log_send, log_recv, mean_send, mean_recv,
    ) = rest
    diffusion, radius, obs_cells, obs_count, obs_value, obs_error = small
    members, fields, width, levels, lat, sites_max = dims
    first = observed_field + 1
    groups = ((observed_field, first), (0, observed_field), (first, fields))
    each = width // n_mem
    chunks = lat // lanes
    radii = radius_range(width)
    classes = distance_classes(width)
    me = lax.axis_index("mem")
    place = lax.axis_index("space")
    right, left = lax.rem(place + 1, n_space), lax.rem(place + n_space - 1, n_space)

    barrier = pltpu.get_barrier_semaphore()
    for side in (left, right):
        pl.semaphore_signal(barrier, inc=1, device_id={"space": side}, device_id_type=MESH)
    for p in range(1, n_mem):
        pl.semaphore_signal(
            barrier, inc=1, device_id={"mem": lax.rem(me + p, n_mem)}, device_id_type=MESH
        )

    load = pltpu.make_async_copy(state, st.at[:, :, 2 : 2 + width], load_sem)
    load.start()
    fetches = []
    for i, (src, dst) in enumerate(zip(small_hbm, small)):
        fetch = pltpu.make_async_copy(src, dst, small_sem.at[i])
        fetch.start()
        fetches.append(fetch)

    pl.semaphore_wait(barrier, 2 + n_mem - 1)

    def halo(g):
        lo, hi, layers, sides = (
            (observed_field, first, 2, ((width - 2, 0), (0, width + 2))),
            (0, observed_field, 1, ((width - 1, 1), (0, width + 2))),
            (0, observed_field, 1, ((width - 2, 0), (1, width + 3))),
            (first, fields, 2, ((width - 2, 0), (0, width + 2))),
        )[g]
        copies = []
        for side, (src, dst) in enumerate(sides):
            copy = pltpu.make_async_remote_copy(
                src_ref=state.at[:, lo:hi, src : src + layers],
                dst_ref=st.at[:, lo:hi, dst : dst + layers],
                send_sem=halo_send.at[g, side],
                recv_sem=halo_recv.at[g, side],
                device_id={"space": (right, left)[side]},
                device_id_type=MESH,
            )
            copy.start()
            copies.append(copy)
        return copies

    halos = [halo(0), halo(1)]

    for fetch in fetches:
        fetch.wait()

    rates = [diffusion[f] * time_step for f in range(fields)]

    def advance(src, wind, m, row, f):
        centre = src[m, f, row]
        east, west = src[m, f, row + 1], src[m, f, row - 1]
        north = pltpu.roll(centre, lat - 1, 1)
        south = pltpu.roll(centre, 1, 1)
        spread = (east + west) + (north + south) - 4.0 * centre
        return centre + (rates[f] * spread - (wind[0] * (east - west) + wind[1] * (north - south)))

    def winds(src, m, row):
        half = 0.5 * time_step
        return src[m, 0, row] * half, src[m, 1, row] * half

    def step_one(m, x, span):
        wind = winds(st, m, x + 2)
        for f in range(*span):
            mid[m, f, x + 1] = advance(st, wind, m, x + 2, f)

    def step_two(m, x, span):
        wind = winds(mid, m, x + 1)
        for f in range(*span):
            value = advance(mid, wind, m, x + 1, f)
            adv[m, f, x] = value
            if f == observed_field:
                column = jnp.mean(value, axis=0, keepdims=True)
                for h in range(chunks):
                    img[m, h, pl.ds(width + x, 1)] = column[:, h * lanes : (h + 1) * lanes]

    def inner(step, low, high, span):
        count = high - low

        @pl.loop(0, members * count, unroll=math.gcd(members * count, 8))
        def _(i):
            step(i // count, low + i % count, span)

    def at_rows(step, rows, span):
        @pl.loop(0, members, unroll=members)
        def _(m):
            for x in rows:
                step(m, x, span)

    edges, inside = (0, width - 1), (1, width - 2)
    beyond = (-1, width)

    load.wait()
    inner(step_one, 1, width - 1, (0, fields))
    inner(step_two, 2, width - 2, (0, fields))

    cell_at = lax.broadcasted_iota(jnp.int32, (width, lat), 0) * lat
    cell_at = cell_at + lax.broadcasted_iota(jnp.int32, (width, lat), 1)
    count = obs_count[0]

    def precision(o):
        valid = jnp.where(o < count, 1.0, 0.0)
        error = jnp.full((width, lat), obs_error[0, o], jnp.float32)
        here = cell_at == obs_cells[0, o]
        return jnp.where(here, valid / (error * error), 0.0)

    def gather_sums(o, carry):
        weight = precision(o)
        return carry[0] + weight, carry[1] + weight * obs_value[0, o]

    zero = jnp.zeros((width, lat), jnp.float32)
    weight_sum, value_sum = lax.fori_loop(0, sites_max, gather_sums, (zero, zero), unroll=4)
    centre_value = jnp.where(
        weight_sum > 0.0, value_sum / jnp.where(weight_sum > 0.0, weight_sum, 1.0), 0.0
    )

    def gather_spread(o, carry):
        away = obs_value[0, o] - centre_value
        return carry + precision(o) * (away * away)

    obs_img[0] = weight_sum
    obs_img[1] = centre_value
    obs_img[2] = lax.fori_loop(0, sites_max, gather_spread, zero, unroll=4)

    level_at = lax.broadcasted_iota(jnp.int32, (levels, lanes), 0)
    level_radius = jnp.zeros((levels, lanes), jnp.int32)
    for z in range(levels):
        level_radius = jnp.where(level_at == z, radius[z], level_radius)
    logs_out[...] = jnp.zeros_like(logs_out)

    for copy in halos[0] + halos[1]:
        copy.wait_recv()
    at_rows(step_one, edges, (0, first))
    at_rows(step_one, beyond, groups[0])
    at_rows(step_two, edges + inside, groups[0])

    own_rows = pl.ds(width, width)
    for m in range(members):
        for h in range(chunks):
            part_lanes = slice(h * lanes, (h + 1) * lanes)
            away = img[m, h, own_rows] - obs_img[1, :, part_lanes]
            img[m, h, own_rows] = obs_img[2, :, part_lanes] + obs_img[0, :, part_lanes] * (away * away)

    img_copies = []
    for side, (dst, target) in enumerate(((0, right), (2 * width, left))):
        copy = pltpu.make_async_remote_copy(
            src_ref=img.at[:, :, width : 2 * width],
            dst_ref=img.at[:, :, dst : dst + width],
            send_sem=img_send.at[side],
            recv_sem=img_recv.at[side],
            device_id={"space": target},
            device_id_type=MESH,
        )
        copy.start()
        img_copies.append(copy)
    halos.append(halo(2))
    halos.append(halo(3))

    def roll_rows(tile):
        rows = pl.ds(tile * width, width)

        @pl.loop(0, members, unroll=members)
        def _(m):
            row = jnp.concatenate([img[m, h, rows] for h in range(chunks)], axis=1)
            for b in range(1, width):
                both = pltpu.roll(row, b, 1) + pltpu.roll(row, lat - b, 1)
                for h in range(chunks):
                    rolled[b - 1, m, h, rows] = both[:, h * lanes : (h + 1) * lanes]

    roll_rows(1)
    at_rows(step_two, inside, groups[1])
    for copy in img_copies:
        copy.wait_recv()
    roll_rows(0)
    roll_rows(2)

    def shifted(m, h, a, b):
        source = img.at[m, h] if b == 0 else rolled.at[b - 1, m, h]
        term = source[pl.ds(width - a, width)]
        return term + source[pl.ds(width + a, width)] if a else term

    @pl.loop(0, chunks, unroll=chunks)
    def _(h):
        logs = []
        for m in range(members):
            sums = [None] * len(radii)
            for distance, pairs in classes:
                total = functools.reduce(jnp.add, [shifted(m, h, a, b) for a, b in pairs])
                for i, reach in enumerate(radii):
                    if distance < reach * reach:
                        taper = 1.0 - distance / (reach * reach)
                        term = (-0.5 * taper * taper) * total
                        sums[i] = term if sums[i] is None else sums[i] + term
            logs.append(sums)
        for i in range(len(radii)):
            best = functools.reduce(jnp.maximum, [logs[m][i] for m in range(members)])
            expo = [jnp.exp(logs[m][i] - best) for m in range(members)]
            total = functools.reduce(jnp.add, expo)
            scale = 1.0 / total
            for m in range(members):
                gain_class[m, i, h] = expo[m] * scale
            local_log = best + jnp.log(total)
            for owner in range(n_mem):
                for j in range(each):
                    x = row_of(owner, j, n_mem, width)
                    logs_out[owner, j, h, pl.ds(i, 1)] = local_log[x : x + 1]

    def expand(read):
        parts = []
        for h in range(chunks):
            value = jnp.broadcast_to(read(0, h), (levels, lanes))
            for i in range(1, len(radii)):
                value = jnp.where(level_radius == radii[i], read(i, h), value)
            parts.append(value)
        return jnp.concatenate(parts, axis=1)

    order = [observed_field] + [f for f in range(fields) if f != observed_field]
    late = 1 if each == 2 else each
    units = [
        ((0, 1), (0, each)),
        ((1, fields), (late, each)),
        ((1, first), (0, late)),
        ((first, fields), (0, late)),
    ]

    def sum_row(u, owner, j):
        x = row_of(owner, j, n_mem, width)
        if u == 0:
            for m in range(members):
                gain[m, x] = expand(lambda i, h: gain_class[m, i, h, pl.ds(x, 1)])
        weights = [gain[m, x] for m in range(members)]
        for k in range(*units[u][0]):
            part[owner, k, j] = functools.reduce(
                jnp.add, [weights[m] * adv[m, order[k], x] for m in range(members)]
            )

    def send(src, dst, send_sem, recv_sem, target):
        copy = pltpu.make_async_remote_copy(
            src_ref=src, dst_ref=dst, send_sem=send_sem, recv_sem=recv_sem,
            device_id={"mem": target}, device_id_type=MESH,
        )
        copy.start()
        return copy

    part_copies = [[] for _ in units]
    peers = list(range(1, n_mem)) + [0]

    def spread(u):
        (lo, hi), (low, high) = units[u]
        if low == high:
            return
        for p in peers:
            owner = lax.rem(me + p, n_mem)
            if u == 0 and p:
                part_copies[u].append(
                    send(logs_out.at[owner], logs_in.at[p], log_send.at[p], log_recv.at[p], owner)
                )
            for j in range(low, high):
                sum_row(u, owner, j)
            if p:
                box = (slice(lo, hi), slice(low, high))
                part_copies[u].append(
                    send(
                        part.at[(owner,) + box], inbox.at[(p,) + box],
                        part_send.at[u, p], part_recv.at[u, p], owner,
                    )
                )

    pieces = [[(0, j, j) for j in range(each)]]
    pieces.append([(g, j, each + 2 * (j - late) + g - 1) for j in range(late, each) for g in (1, 2)])
    pieces.append([(1, j, 3 * each - 2 * late + j) for j in range(late)])
    pieces.append([(2, j, 3 * each - late + j) for j in range(late)])
    mean_copies = []

    def send_mean(piece, p):
        g, j, n = piece
        lo, hi = groups[g]
        block = mean.at[lo:hi, pl.ds(row_of(me, j, n_mem, width), 1)]
        return send(block, block, mean_send.at[n, p], mean_recv.at[n, p], lax.rem(me + p, n_mem))

    def merge(u):
        (lo, hi), (low, high) = units[u]
        if low == high:
            return
        for copy in part_copies[u]:
            copy.wait_recv()
        for j in range(low, high):
            if u == 0:
                logs = [logs_out[me, j]] + [logs_in[p, j] for p in range(1, n_mem)]
                best = functools.reduce(jnp.maximum, logs)
                expo = [jnp.exp(value - best) for value in logs]
                scale = 1.0 / functools.reduce(jnp.add, expo)
                for p in range(n_mem):
                    share_class[p, j] = expo[p] * scale
                for p in range(n_mem):
                    share[p, j] = expand(lambda i, h: share_class[p, j, h, pl.ds(i, 1)])
            weights = [share[p, j] for p in range(n_mem)]
            for k in range(lo, hi):
                total = weights[0] * part[me, k, j]
                for p in range(1, n_mem):
                    total = total + weights[p] * inbox[p, k, j]
                mean[order[k], row_of(me, j, n_mem, width)] = total
        for piece in pieces[u]:
            for p in range(1, n_mem):
                mean_copies.append(send_mean(piece, p))

    def late_winds():
        for copy in halos[2]:
            copy.wait_recv()
        at_rows(step_one, beyond, groups[1])
        at_rows(step_two, edges, groups[1])
        spread(2)

    def late_rest():
        for copy in halos[3]:
            copy.wait_recv()
        at_rows(step_one, beyond + edges, groups[2])
        at_rows(step_two, edges + inside, groups[2])
        spread(3)

    spread(0)
    spread(1)
    late_winds()
    merge(0)
    late_rest()
    merge(1)
    merge(2)
    merge(3)

    for copy in mean_copies:
        copy.wait_recv()
    for copy in sum(halos, []) + img_copies + sum(part_copies, []) + mean_copies:
        copy.wait_send()


def blend(adv, mean, out, staged, sems):
    members, fields = adv.shape[:2]
    copies = []
    for m in range(members):
        for f in range(fields):
            staged[m, f] = adv[m, f] + blend_share * (mean[f] - adv[m, f])
            copy = pltpu.make_async_copy(staged.at[m, f], out.at[m, f], sems.at[m, f])
            copy.start()
            copies.append(copy)
    for copy in copies:
        copy.wait()


def local(n_mem, n_space, state, diffusion, radius, obs_cells, obs_count, obs_value, obs_error):
    members, fields, width, levels, lat = state.shape
    sites_max = obs_cells.shape[1]
    dims = (members, fields, width, levels, lat, sites_max)
    each = width // n_mem
    chunks = lat // lanes
    n_radii = len(radius_range(width))
    slots = -(-n_radii // sublanes) * sublanes
    n_pieces = 3 * each
    dma = pltpu.SemaphoreType.DMA

    def vmem(*shape):
        return pltpu.VMEM(shape, jnp.float32)

    small = (diffusion, radius, obs_cells, obs_count, obs_value, obs_error)
    held = [
        value if value.size == 1 else pltpu.with_memory_space_constraint(value, pltpu.HBM)
        for value in (state, *small)
    ]
    hbm = pl.BlockSpec(memory_space=pltpu.HBM)
    adv, mean = pl.pallas_call(
        functools.partial(kernel, n_mem, n_space, dims),
        out_shape=[
            pltpu.VMEM(state.shape, jnp.float32),
            pltpu.VMEM(state.shape[1:], jnp.float32),
        ],
        in_specs=[hbm] * 7,
        out_specs=[pl.BlockSpec(memory_space=pltpu.VMEM)] * 2,
        scratch_shapes=[pltpu.SMEM(value.shape, value.dtype) for value in small]
        + [
            vmem(members, fields, width + 4, levels, lat),
            vmem(members, fields, width + 2, levels, lat),
            vmem(3, width, lat),
            vmem(members, chunks, 3 * width, lanes),
            vmem(width - 1, members, chunks, 3 * width, lanes),
            vmem(members, n_radii, chunks, width, lanes),
            vmem(members, width, levels, lat),
            vmem(n_mem, fields, each, levels, lat),
            vmem(n_mem, fields, each, levels, lat),
            vmem(n_mem, each, chunks, slots, lanes),
            vmem(n_mem, each, chunks, slots, lanes),
            vmem(n_mem, each, chunks, slots, lanes),
            vmem(n_mem, each, levels, lat),
            dma((len(small),)),
            dma,
            dma((4, 2)),
            dma((4, 2)),
            dma((2,)),
            dma((2,)),
            dma((4, n_mem)),
            dma((4, n_mem)),
            dma((n_mem,)),
            dma((n_mem,)),
            dma((n_pieces, n_mem)),
            dma((n_pieces, n_mem)),
        ],
        compiler_params=pltpu.CompilerParams(
            collective_id=0, has_side_effects=True, vmem_limit_bytes=24 * 2**20
        ),
    )(*held)
    return pl.pallas_call(
        blend,
        out_shape=jax.ShapeDtypeStruct(state.shape, jnp.float32),
        in_specs=[pl.BlockSpec(memory_space=pltpu.VMEM)] * 2,
        out_specs=pl.BlockSpec(memory_space=pltpu.HBM),
        scratch_shapes=[vmem(*state.shape), dma((members, fields))],
        compiler_params=pltpu.CompilerParams(vmem_limit_bytes=16 * 2**20),
    )(*[pltpu.with_memory_space_constraint(value, pltpu.VMEM) for value in (adv, mean)])


def solution(mesh):
    return jax.shard_map(
        functools.partial(local, mesh.shape["mem"], mesh.shape["space"]),
        mesh=mesh,
        in_specs=(
            P("mem", None, "space", None, None),
            P(),
            P(),
            P("space", None),
            P("space"),
            P("space", None),
            P("space", None),
        ),
        out_specs=P("mem", None, "space", None, None),
        check_vma=False,
    )
```

```python
import functools
import math

import jax
import jax.numpy as jnp
from jax import lax
from jax.experimental import pallas as pl
from jax.experimental.pallas import tpu as pltpu
from jax.sharding import PartitionSpec as P

time_step = 0.2
blend_share = 0.5
observed_field = 2
lanes, sublanes = 128, 8
MESH = pl.DeviceIdType.MESH


def distance_classes(reach):
    classes = {}
    for a in range(reach):
        for b in range(reach):
            if a * a + b * b < reach * reach:
                classes.setdefault(a * a + b * b, []).append((a, b))
    return sorted(classes.items())


def radius_range(width):
    return range(width // 2, width + 1)


def row_of(owner, j, n_mem, width):
    each = width // n_mem
    if each != 2:
        return owner * each + j
    half = n_mem // 2
    return half + owner if j else owner + (owner // half) * (width - n_mem)


def kernel(
    n_mem, n_space, dims,
    state, *rest,
):
    small_hbm, rest = rest[:6], rest[6:]
    adv, mean = rest[:2]
    small, rest = rest[2:8], rest[8:]
    (
        st, mid, obs_img, img, rolled, gain_class, gain, part, inbox, logs_out, logs_in, share_class, share,
        small_sem, load_sem, halo_send, halo_recv, img_send, img_recv,
        part_send, part_recv, log_send, log_recv, mean_send, mean_recv,
    ) = rest
    diffusion, radius, obs_cells, obs_count, obs_value, obs_error = small
    members, fields, width, levels, lat, sites_max = dims
    first = observed_field + 1
    groups = ((observed_field, first), (0, observed_field), (first, fields))
    each = width // n_mem
    chunks = lat // lanes
    radii = radius_range(width)
    classes = distance_classes(width)
    me = lax.axis_index("mem")
    place = lax.axis_index("space")
    right, left = lax.rem(place + 1, n_space), lax.rem(place + n_space - 1, n_space)

    barrier = pltpu.get_barrier_semaphore()
    for side in (left, right):
        pl.semaphore_signal(barrier, inc=1, device_id={"space": side}, device_id_type=MESH)
    for p in range(1, n_mem):
        pl.semaphore_signal(
            barrier, inc=1, device_id={"mem": lax.rem(me + p, n_mem)}, device_id_type=MESH
        )

    load = pltpu.make_async_copy(state, st.at[:, :, 2 : 2 + width], load_sem)
    load.start()
    fetches = []
    for i, (src, dst) in enumerate(zip(small_hbm, small)):
        fetch = pltpu.make_async_copy(src, dst, small_sem.at[i])
        fetch.start()
        fetches.append(fetch)

    pl.semaphore_wait(barrier, 2 + n_mem - 1)

    singles = [(m, m + 1) for m in range(members)]

    def halo(g, low=0, high=members):
        lo, hi, layers, sides = (
            (observed_field, first, 2, ((width - 2, 0), (0, width + 2))),
            (0, observed_field, 1, ((width - 1, 1), (0, width + 2))),
            (0, observed_field, 1, ((width - 2, 0), (1, width + 3))),
            (first, fields, 2, ((width - 2, 0), (0, width + 2))),
        )[g]
        copies = []
        for side, (src, dst) in enumerate(sides):
            copy = pltpu.make_async_remote_copy(
                src_ref=state.at[low:high, lo:hi, src : src + layers],
                dst_ref=st.at[low:high, lo:hi, dst : dst + layers],
                send_sem=halo_send.at[g, low, side],
                recv_sem=halo_recv.at[g, low, side],
                device_id={"space": (right, left)[side]},
                device_id_type=MESH,
            )
            copy.start()
            copies.append(copy)
        return copies

    first_halos = [halo(0, *span_m) + halo(1, *span_m) for span_m in singles]

    for fetch in fetches:
        fetch.wait()

    rates = [diffusion[f] * time_step for f in range(fields)]

    def advance(src, wind, m, row, f):
        centre = src[m, f, row]
        east, west = src[m, f, row + 1], src[m, f, row - 1]
        north = pltpu.roll(centre, lat - 1, 1)
        south = pltpu.roll(centre, 1, 1)
        spread = (east + west) + (north + south) - 4.0 * centre
        return centre + (rates[f] * spread - (wind[0] * (east - west) + wind[1] * (north - south)))

    def winds(src, m, row):
        half = 0.5 * time_step
        return src[m, 0, row] * half, src[m, 1, row] * half

    def step_one(m, x, span):
        wind = winds(st, m, x + 2)
        for f in range(*span):
            mid[m, f, x + 1] = advance(st, wind, m, x + 2, f)

    def step_two(m, x, span):
        wind = winds(mid, m, x + 1)
        for f in range(*span):
            value = advance(mid, wind, m, x + 1, f)
            adv[m, f, x] = value
            if f == observed_field:
                column = jnp.mean(value, axis=0, keepdims=True)
                for h in range(chunks):
                    img[m, h, pl.ds(width + x, 1)] = column[:, h * lanes : (h + 1) * lanes]

    def inner(step, low, high, span):
        count = high - low

        @pl.loop(0, members * count, unroll=math.gcd(members * count, 8))
        def _(i):
            step(i // count, low + i % count, span)

    def at_rows(step, rows, span, low=0, high=members):
        @pl.loop(low, high, unroll=high - low)
        def _(m):
            for x in rows:
                step(m, x, span)

    edges, inside = (0, width - 1), (1, width - 2)
    beyond = (-1, width)

    load.wait()
    inner(step_one, 1, width - 1, (0, fields))
    inner(step_two, 2, width - 2, (0, fields))

    cell_at = lax.broadcasted_iota(jnp.int32, (width, lat), 0) * lat
    cell_at = cell_at + lax.broadcasted_iota(jnp.int32, (width, lat), 1)
    count = obs_count[0]

    def precision(o):
        valid = jnp.where(o < count, 1.0, 0.0)
        error = jnp.full((width, lat), obs_error[0, o], jnp.float32)
        here = cell_at == obs_cells[0, o]
        return jnp.where(here, valid / (error * error), 0.0)

    def gather_sums(o, carry):
        weight = precision(o)
        return carry[0] + weight, carry[1] + weight * obs_value[0, o]

    zero = jnp.zeros((width, lat), jnp.float32)
    weight_sum, value_sum = lax.fori_loop(0, sites_max, gather_sums, (zero, zero), unroll=4)
    centre_value = jnp.where(
        weight_sum > 0.0, value_sum / jnp.where(weight_sum > 0.0, weight_sum, 1.0), 0.0
    )

    def gather_spread(o, carry):
        away = obs_value[0, o] - centre_value
        return carry + precision(o) * (away * away)

    obs_img[0] = weight_sum
    obs_img[1] = centre_value
    obs_img[2] = lax.fori_loop(0, sites_max, gather_spread, zero, unroll=4)

    level_at = lax.broadcasted_iota(jnp.int32, (levels, lanes), 0)
    level_radius = jnp.zeros((levels, lanes), jnp.int32)
    for z in range(levels):
        level_radius = jnp.where(level_at == z, radius[z], level_radius)
    logs_out[...] = jnp.zeros_like(logs_out)

    own_rows = pl.ds(width, width)
    img_copies = []
    for i, span_m in enumerate(singles):
        for copy in first_halos[i]:
            copy.wait_recv()
        at_rows(step_one, edges, (0, first), *span_m)
        at_rows(step_one, beyond, groups[0], *span_m)
        at_rows(step_two, edges + inside, groups[0], *span_m)
        for m in range(*span_m):
            for h in range(chunks):
                part_lanes = slice(h * lanes, (h + 1) * lanes)
                away = img[m, h, own_rows] - obs_img[1, :, part_lanes]
                img[m, h, own_rows] = obs_img[2, :, part_lanes] + obs_img[0, :, part_lanes] * (away * away)
        copies = []
        for side, (dst, target) in enumerate(((0, right), (2 * width, left))):
            copy = pltpu.make_async_remote_copy(
                src_ref=img.at[span_m[0] : span_m[1], :, width : 2 * width],
                dst_ref=img.at[span_m[0] : span_m[1], :, dst : dst + width],
                send_sem=img_send.at[i, side],
                recv_sem=img_recv.at[i, side],
                device_id={"space": target},
                device_id_type=MESH,
            )
            copy.start()
            copies.append(copy)
        img_copies.append(copies)
    rest_halo = halo(3)
    winds_halo = halo(2)

    def roll_rows(tile, low=0, high=members):
        rows = pl.ds(tile * width, width)

        @pl.loop(low, high, unroll=high - low)
        def _(m):
            row = jnp.concatenate([img[m, h, rows] for h in range(chunks)], axis=1)
            for b in range(1, width):
                both = pltpu.roll(row, b, 1) + pltpu.roll(row, lat - b, 1)
                for h in range(chunks):
                    rolled[b - 1, m, h, rows] = both[:, h * lanes : (h + 1) * lanes]

    roll_rows(1)
    at_rows(step_two, inside, groups[1])
    for copies, span_m in zip(img_copies, singles):
        for copy in copies:
            copy.wait_recv()
        roll_rows(0, *span_m)
        roll_rows(2, *span_m)

    def shifted(m, h, a, b):
        source = img.at[m, h] if b == 0 else rolled.at[b - 1, m, h]
        term = source[pl.ds(width - a, width)]
        return term + source[pl.ds(width + a, width)] if a else term

    @pl.loop(0, chunks, unroll=chunks)
    def _(h):
        logs = []
        for m in range(members):
            sums = [None] * len(radii)
            for distance, pairs in classes:
                total = functools.reduce(jnp.add, [shifted(m, h, a, b) for a, b in pairs])
                for i, reach in enumerate(radii):
                    if distance < reach * reach:
                        taper = 1.0 - distance / (reach * reach)
                        term = (-0.5 * taper * taper) * total
                        sums[i] = term if sums[i] is None else sums[i] + term
            logs.append(sums)
        for i in range(len(radii)):
            best = functools.reduce(jnp.maximum, [logs[m][i] for m in range(members)])
            expo = [jnp.exp(logs[m][i] - best) for m in range(members)]
            total = functools.reduce(jnp.add, expo)
            scale = 1.0 / total
            for m in range(members):
                gain_class[m, i, h] = expo[m] * scale
            local_log = best + jnp.log(total)
            for owner in range(n_mem):
                for j in range(each):
                    x = row_of(owner, j, n_mem, width)
                    logs_out[owner, j, h, pl.ds(i, 1)] = local_log[x : x + 1]

    def expand(read):
        parts = []
        for h in range(chunks):
            value = jnp.broadcast_to(read(0, h), (levels, lanes))
            for i in range(1, len(radii)):
                value = jnp.where(level_radius == radii[i], read(i, h), value)
            parts.append(value)
        return jnp.concatenate(parts, axis=1)

    order = [observed_field] + [f for f in range(fields) if f != observed_field]
    late = 1 if each == 2 else each
    units = [
        ((0, 1), (0, each)),
        ((1, fields), (late, each)),
        ((1, first), (0, late)),
        ((first, fields), (0, late)),
    ]

    def sum_row(u, owner, j):
        x = row_of(owner, j, n_mem, width)
        if u == 0:
            for m in range(members):
                gain[m, x] = expand(lambda i, h: gain_class[m, i, h, pl.ds(x, 1)])
        weights = [gain[m, x] for m in range(members)]
        for k in range(*units[u][0]):
            part[owner, k, j] = functools.reduce(
                jnp.add, [weights[m] * adv[m, order[k], x] for m in range(members)]
            )

    def send(src, dst, send_sem, recv_sem, target):
        copy = pltpu.make_async_remote_copy(
            src_ref=src, dst_ref=dst, send_sem=send_sem, recv_sem=recv_sem,
            device_id={"mem": target}, device_id_type=MESH,
        )
        copy.start()
        return copy

    part_copies = [[] for _ in units]
    peers = list(range(1, n_mem)) + [0]

    def spread(u):
        (lo, hi), (low, high) = units[u]
        if low == high:
            return
        for p in peers:
            owner = lax.rem(me + p, n_mem)
            if u == 0 and p:
                part_copies[u].append(
                    send(logs_out.at[owner], logs_in.at[p], log_send.at[p], log_recv.at[p], owner)
                )
            for j in range(low, high):
                sum_row(u, owner, j)
            if p:
                box = (slice(lo, hi), slice(low, high))
                part_copies[u].append(
                    send(
                        part.at[(owner,) + box], inbox.at[(p,) + box],
                        part_send.at[u, p], part_recv.at[u, p], owner,
                    )
                )

    pieces = [[(0, j, j) for j in range(each)]]
    pieces.append([(g, j, each + 2 * (j - late) + g - 1) for j in range(late, each) for g in (1, 2)])
    pieces.append([(1, j, 3 * each - 2 * late + j) for j in range(late)])
    pieces.append([(2, j, 3 * each - late + j) for j in range(late)])
    mean_copies = []

    def send_mean(piece, p):
        g, j, n = piece
        lo, hi = groups[g]
        block = mean.at[lo:hi, pl.ds(row_of(me, j, n_mem, width), 1)]
        return send(block, block, mean_send.at[n, p], mean_recv.at[n, p], lax.rem(me + p, n_mem))

    def merge(u):
        (lo, hi), (low, high) = units[u]
        if low == high:
            return
        for copy in part_copies[u]:
            copy.wait_recv()
        for j in range(low, high):
            if u == 0:
                logs = [logs_out[me, j]] + [logs_in[p, j] for p in range(1, n_mem)]
                best = functools.reduce(jnp.maximum, logs)
                expo = [jnp.exp(value - best) for value in logs]
                scale = 1.0 / functools.reduce(jnp.add, expo)
                for p in range(n_mem):
                    share_class[p, j] = expo[p] * scale
                for p in range(n_mem):
                    share[p, j] = expand(lambda i, h: share_class[p, j, h, pl.ds(i, 1)])
            weights = [share[p, j] for p in range(n_mem)]
            for k in range(lo, hi):
                total = weights[0] * part[me, k, j]
                for p in range(1, n_mem):
                    total = total + weights[p] * inbox[p, k, j]
                mean[order[k], row_of(me, j, n_mem, width)] = total
        for piece in pieces[u]:
            for p in range(1, n_mem):
                mean_copies.append(send_mean(piece, p))

    def late_winds():
        for copy in winds_halo:
            copy.wait_recv()
        at_rows(step_one, beyond, groups[1])
        at_rows(step_two, edges, groups[1])
        spread(2)

    def late_rest():
        for copy in rest_halo:
            copy.wait_recv()
        at_rows(step_one, beyond + edges, groups[2])
        at_rows(step_two, edges + inside, groups[2])
        spread(3)

    spread(0)
    spread(1)
    late_rest()
    merge(0)
    late_winds()
    merge(1)
    merge(3)
    merge(2)

    for copy in mean_copies:
        copy.wait_recv()
    halos = sum(first_halos, []) + winds_halo + rest_halo
    for copy in halos + sum(img_copies, []) + sum(part_copies, []) + mean_copies:
        copy.wait_send()


def blend(adv, mean, out, staged, sems):
    members, fields = adv.shape[:2]
    copies = []
    for m in range(members):
        for f in range(fields):
            staged[m, f] = adv[m, f] + blend_share * (mean[f] - adv[m, f])
            copy = pltpu.make_async_copy(staged.at[m, f], out.at[m, f], sems.at[m, f])
            copy.start()
            copies.append(copy)
    for copy in copies:
        copy.wait()


def local(n_mem, n_space, state, diffusion, radius, obs_cells, obs_count, obs_value, obs_error):
    members, fields, width, levels, lat = state.shape
    sites_max = obs_cells.shape[1]
    dims = (members, fields, width, levels, lat, sites_max)
    each = width // n_mem
    chunks = lat // lanes
    n_radii = len(radius_range(width))
    slots = -(-n_radii // sublanes) * sublanes
    n_pieces = 3 * each
    dma = pltpu.SemaphoreType.DMA

    def vmem(*shape):
        return pltpu.VMEM(shape, jnp.float32)

    small = (diffusion, radius, obs_cells, obs_count, obs_value, obs_error)
    held = [
        value if value.size == 1 else pltpu.with_memory_space_constraint(value, pltpu.HBM)
        for value in (state, *small)
    ]
    hbm = pl.BlockSpec(memory_space=pltpu.HBM)
    adv, mean = pl.pallas_call(
        functools.partial(kernel, n_mem, n_space, dims),
        out_shape=[
            pltpu.VMEM(state.shape, jnp.float32),
            pltpu.VMEM(state.shape[1:], jnp.float32),
        ],
        in_specs=[hbm] * 7,
        out_specs=[pl.BlockSpec(memory_space=pltpu.VMEM)] * 2,
        scratch_shapes=[pltpu.SMEM(value.shape, value.dtype) for value in small]
        + [
            vmem(members, fields, width + 4, levels, lat),
            vmem(members, fields, width + 2, levels, lat),
            vmem(3, width, lat),
            vmem(members, chunks, 3 * width, lanes),
            vmem(width - 1, members, chunks, 3 * width, lanes),
            vmem(members, n_radii, chunks, width, lanes),
            vmem(members, width, levels, lat),
            vmem(n_mem, fields, each, levels, lat),
            vmem(n_mem, fields, each, levels, lat),
            vmem(n_mem, each, chunks, slots, lanes),
            vmem(n_mem, each, chunks, slots, lanes),
            vmem(n_mem, each, chunks, slots, lanes),
            vmem(n_mem, each, levels, lat),
            dma((len(small),)),
            dma,
            dma((4, members, 2)),
            dma((4, members, 2)),
            dma((members, 2)),
            dma((members, 2)),
            dma((4, n_mem)),
            dma((4, n_mem)),
            dma((n_mem,)),
            dma((n_mem,)),
            dma((n_pieces, n_mem)),
            dma((n_pieces, n_mem)),
        ],
        compiler_params=pltpu.CompilerParams(
            collective_id=0, has_side_effects=True, vmem_limit_bytes=24 * 2**20
        ),
    )(*held)
    return pl.pallas_call(
        blend,
        out_shape=jax.ShapeDtypeStruct(state.shape, jnp.float32),
        in_specs=[pl.BlockSpec(memory_space=pltpu.VMEM)] * 2,
        out_specs=pl.BlockSpec(memory_space=pltpu.HBM),
        scratch_shapes=[vmem(*state.shape), dma((members, fields))],
        compiler_params=pltpu.CompilerParams(vmem_limit_bytes=16 * 2**20),
    )(*[pltpu.with_memory_space_constraint(value, pltpu.VMEM) for value in (adv, mean)])


def solution(mesh):
    return jax.shard_map(
        functools.partial(local, mesh.shape["mem"], mesh.shape["space"]),
        mesh=mesh,
        in_specs=(
            P("mem", None, "space", None, None),
            P(),
            P(),
            P("space", None),
            P("space"),
            P("space", None),
            P("space", None),
        ),
        out_specs=P("mem", None, "space", None, None),
        check_vma=False,
    )
```

```python
import functools
import math

import jax
import jax.numpy as jnp
from jax import lax
from jax.experimental import pallas as pl
from jax.experimental.pallas import tpu as pltpu
from jax.sharding import PartitionSpec as P

time_step = 0.2
blend_share = 0.5
observed_field = 2
lanes, sublanes = 128, 8
MESH = pl.DeviceIdType.MESH


def distance_classes(reach):
    classes = {}
    for a in range(reach):
        for b in range(reach):
            if a * a + b * b < reach * reach:
                classes.setdefault(a * a + b * b, []).append((a, b))
    return sorted(classes.items())


def radius_range(width):
    return range(width // 2, width + 1)


def row_of(owner, j, n_mem, width):
    each = width // n_mem
    if each != 2:
        return owner * each + j
    half = n_mem // 2
    return half + owner if j else owner + (owner // half) * (width - n_mem)


def kernel(
    n_mem, n_space, dims,
    state, *rest,
):
    small_hbm, rest = rest[:6], rest[6:]
    adv, mean = rest[:2]
    small, rest = rest[2:8], rest[8:]
    (
        st, mid, obs_img, img, rolled, gain_class, gain, part, inbox, logs_out, logs_in, share_class, share,
        small_sem, load_sem, halo_send, halo_recv, img_send, img_recv,
        part_send, part_recv, log_send, log_recv, mean_send, mean_recv,
    ) = rest
    diffusion, radius, obs_cells, obs_count, obs_value, obs_error = small
    members, fields, width, levels, lat, sites_max = dims
    first = observed_field + 1
    groups = ((observed_field, first), (0, observed_field), (first, fields))
    each = width // n_mem
    chunks = lat // lanes
    radii = radius_range(width)
    classes = distance_classes(width)
    me = lax.axis_index("mem")
    place = lax.axis_index("space")
    right, left = lax.rem(place + 1, n_space), lax.rem(place + n_space - 1, n_space)

    barrier = pltpu.get_barrier_semaphore()
    for side in (left, right):
        pl.semaphore_signal(barrier, inc=1, device_id={"space": side}, device_id_type=MESH)
    for p in range(1, n_mem):
        pl.semaphore_signal(
            barrier, inc=1, device_id={"mem": lax.rem(me + p, n_mem)}, device_id_type=MESH
        )

    load = pltpu.make_async_copy(state, st.at[:, :, 2 : 2 + width], load_sem)
    load.start()
    fetches = []
    for i, (src, dst) in enumerate(zip(small_hbm, small)):
        fetch = pltpu.make_async_copy(src, dst, small_sem.at[i])
        fetch.start()
        fetches.append(fetch)

    pl.semaphore_wait(barrier, 2 + n_mem - 1)

    singles = [(m, m + 1) for m in range(members)]

    def halo(g, low=0, high=members):
        lo, hi, layers, sides = (
            (observed_field, first, 2, ((width - 2, 0), (0, width + 2))),
            (0, observed_field, 1, ((width - 1, 1), (0, width + 2))),
            (0, observed_field, 1, ((width - 2, 0), (1, width + 3))),
            (first, fields, 2, ((width - 2, 0), (0, width + 2))),
        )[g]
        copies = []
        for side, (src, dst) in enumerate(sides):
            copy = pltpu.make_async_remote_copy(
                src_ref=state.at[low:high, lo:hi, src : src + layers],
                dst_ref=st.at[low:high, lo:hi, dst : dst + layers],
                send_sem=halo_send.at[g, low, side],
                recv_sem=halo_recv.at[g, low, side],
                device_id={"space": (right, left)[side]},
                device_id_type=MESH,
            )
            copy.start()
            copies.append(copy)
        return copies

    first_halos = [halo(0, *span_m) + halo(1, *span_m) for span_m in singles]

    for fetch in fetches:
        fetch.wait()

    rates = [diffusion[f] * time_step for f in range(fields)]

    def advance(src, wind, m, row, f):
        centre = src[m, f, row]
        east, west = src[m, f, row + 1], src[m, f, row - 1]
        north = pltpu.roll(centre, lat - 1, 1)
        south = pltpu.roll(centre, 1, 1)
        spread = (east + west) + (north + south) - 4.0 * centre
        return centre + (rates[f] * spread - (wind[0] * (east - west) + wind[1] * (north - south)))

    def winds(src, m, row):
        half = 0.5 * time_step
        return src[m, 0, row] * half, src[m, 1, row] * half

    def step_one(m, x, span):
        wind = winds(st, m, x + 2)
        for f in range(*span):
            mid[m, f, x + 1] = advance(st, wind, m, x + 2, f)

    def step_two(m, x, span):
        wind = winds(mid, m, x + 1)
        for f in range(*span):
            value = advance(mid, wind, m, x + 1, f)
            adv[m, f, x] = value
            if f == observed_field:
                column = jnp.mean(value, axis=0, keepdims=True)
                for h in range(chunks):
                    img[m, h, pl.ds(width + x, 1)] = column[:, h * lanes : (h + 1) * lanes]

    def inner(step, low, high, span):
        count = high - low

        @pl.loop(0, members * count, unroll=math.gcd(members * count, 8))
        def _(i):
            step(i // count, low + i % count, span)

    def at_rows(step, rows, span, low=0, high=members):
        @pl.loop(low, high, unroll=high - low)
        def _(m):
            for x in rows:
                step(m, x, span)

    edges, inside = (0, width - 1), (1, width - 2)
    beyond = (-1, width)

    load.wait()
    inner(step_one, 1, width - 1, (0, fields))
    inner(step_two, 2, width - 2, (0, fields))

    cell_at = lax.broadcasted_iota(jnp.int32, (width, lat), 0) * lat
    cell_at = cell_at + lax.broadcasted_iota(jnp.int32, (width, lat), 1)
    count = obs_count[0]

    def precision(o):
        valid = jnp.where(o < count, 1.0, 0.0)
        error = jnp.full((width, lat), obs_error[0, o], jnp.float32)
        here = cell_at == obs_cells[0, o]
        return jnp.where(here, valid / (error * error), 0.0)

    def gather_sums(o, carry):
        weight = precision(o)
        return carry[0] + weight, carry[1] + weight * obs_value[0, o]

    zero = jnp.zeros((width, lat), jnp.float32)
    weight_sum, value_sum = lax.fori_loop(0, sites_max, gather_sums, (zero, zero), unroll=4)
    centre_value = jnp.where(
        weight_sum > 0.0, value_sum / jnp.where(weight_sum > 0.0, weight_sum, 1.0), 0.0
    )

    def gather_spread(o, carry):
        away = obs_value[0, o] - centre_value
        return carry + precision(o) * (away * away)

    obs_img[0] = weight_sum
    obs_img[1] = centre_value
    obs_img[2] = lax.fori_loop(0, sites_max, gather_spread, zero, unroll=4)

    level_at = lax.broadcasted_iota(jnp.int32, (levels, lanes), 0)
    level_radius = jnp.zeros((levels, lanes), jnp.int32)
    for z in range(levels):
        level_radius = jnp.where(level_at == z, radius[z], level_radius)
    logs_out[...] = jnp.zeros_like(logs_out)

    own_rows = pl.ds(width, width)
    img_copies = []
    for i, span_m in enumerate(singles):
        for copy in first_halos[i]:
            copy.wait_recv()
        at_rows(step_one, edges, (0, first), *span_m)
        at_rows(step_one, beyond, groups[0], *span_m)
        at_rows(step_two, edges + inside, groups[0], *span_m)
        for m in range(*span_m):
            for h in range(chunks):
                part_lanes = slice(h * lanes, (h + 1) * lanes)
                away = img[m, h, own_rows] - obs_img[1, :, part_lanes]
                img[m, h, own_rows] = obs_img[2, :, part_lanes] + obs_img[0, :, part_lanes] * (away * away)
        copies = []
        for side, (dst, target) in enumerate(((0, right), (2 * width, left))):
            copy = pltpu.make_async_remote_copy(
                src_ref=img.at[span_m[0] : span_m[1], :, width : 2 * width],
                dst_ref=img.at[span_m[0] : span_m[1], :, dst : dst + width],
                send_sem=img_send.at[i, side],
                recv_sem=img_recv.at[i, side],
                device_id={"space": target},
                device_id_type=MESH,
            )
            copy.start()
            copies.append(copy)
        img_copies.append(copies)
    late_step = 2 - members % 2
    late_spans = [(m, m + late_step) for m in range(0, members, late_step)]
    rest_halos = [halo(3, *span_m) for span_m in late_spans]
    winds_halo = halo(2)

    def roll_rows(tile, low=0, high=members):
        rows = pl.ds(tile * width, width)

        @pl.loop(low, high, unroll=high - low)
        def _(m):
            row = jnp.concatenate([img[m, h, rows] for h in range(chunks)], axis=1)
            for b in range(1, width):
                both = pltpu.roll(row, b, 1) + pltpu.roll(row, lat - b, 1)
                for h in range(chunks):
                    rolled[b - 1, m, h, rows] = both[:, h * lanes : (h + 1) * lanes]

    roll_rows(1)
    at_rows(step_two, inside, groups[1])
    for copies, span_m in zip(img_copies, singles):
        for copy in copies:
            copy.wait_recv()
        roll_rows(0, *span_m)
        roll_rows(2, *span_m)

    def shifted(m, h, a, b):
        source = img.at[m, h] if b == 0 else rolled.at[b - 1, m, h]
        term = source[pl.ds(width - a, width)]
        return term + source[pl.ds(width + a, width)] if a else term

    @pl.loop(0, chunks, unroll=chunks)
    def _(h):
        logs = []
        for m in range(members):
            sums = [None] * len(radii)
            for distance, pairs in classes:
                total = functools.reduce(jnp.add, [shifted(m, h, a, b) for a, b in pairs])
                for i, reach in enumerate(radii):
                    if distance < reach * reach:
                        taper = 1.0 - distance / (reach * reach)
                        term = (-0.5 * taper * taper) * total
                        sums[i] = term if sums[i] is None else sums[i] + term
            logs.append(sums)
        for i in range(len(radii)):
            best = functools.reduce(jnp.maximum, [logs[m][i] for m in range(members)])
            expo = [jnp.exp(logs[m][i] - best) for m in range(members)]
            total = functools.reduce(jnp.add, expo)
            scale = 1.0 / total
            for m in range(members):
                gain_class[m, i, h] = expo[m] * scale
            local_log = best + jnp.log(total)
            for owner in range(n_mem):
                for j in range(each):
                    x = row_of(owner, j, n_mem, width)
                    logs_out[owner, j, h, pl.ds(i, 1)] = local_log[x : x + 1]

    def expand(read):
        parts = []
        for h in range(chunks):
            value = jnp.broadcast_to(read(0, h), (levels, lanes))
            for i in range(1, len(radii)):
                value = jnp.where(level_radius == radii[i], read(i, h), value)
            parts.append(value)
        return jnp.concatenate(parts, axis=1)

    order = [observed_field] + [f for f in range(fields) if f != observed_field]
    late = 1 if each == 2 else each
    units = [
        ((0, 1), (0, each)),
        ((1, fields), (late, each)),
        ((1, first), (0, late)),
        ((first, fields), (0, late)),
    ]

    def sum_row(u, owner, j):
        x = row_of(owner, j, n_mem, width)
        if u == 0:
            for m in range(members):
                gain[m, x] = expand(lambda i, h: gain_class[m, i, h, pl.ds(x, 1)])
        weights = [gain[m, x] for m in range(members)]
        for k in range(*units[u][0]):
            part[owner, k, j] = functools.reduce(
                jnp.add, [weights[m] * adv[m, order[k], x] for m in range(members)]
            )

    def send(src, dst, send_sem, recv_sem, target):
        copy = pltpu.make_async_remote_copy(
            src_ref=src, dst_ref=dst, send_sem=send_sem, recv_sem=recv_sem,
            device_id={"mem": target}, device_id_type=MESH,
        )
        copy.start()
        return copy

    part_copies = [[] for _ in units]
    peers = list(range(1, n_mem)) + [0]

    def spread(u):
        (lo, hi), (low, high) = units[u]
        if low == high:
            return
        for p in peers:
            owner = lax.rem(me + p, n_mem)
            if u == 0 and p:
                part_copies[u].append(
                    send(logs_out.at[owner], logs_in.at[p], log_send.at[p], log_recv.at[p], owner)
                )
            for j in range(low, high):
                sum_row(u, owner, j)
            if p:
                box = (slice(lo, hi), slice(low, high))
                part_copies[u].append(
                    send(
                        part.at[(owner,) + box], inbox.at[(p,) + box],
                        part_send.at[u, p], part_recv.at[u, p], owner,
                    )
                )

    pieces = [[(0, j, j) for j in range(each)]]
    pieces.append([(g, j, each + 2 * (j - late) + g - 1) for j in range(late, each) for g in (1, 2)])
    pieces.append([(1, j, 3 * each - 2 * late + j) for j in range(late)])
    pieces.append([(2, j, 3 * each - late + j) for j in range(late)])
    mean_copies = []

    def send_mean(piece, p):
        g, j, n = piece
        lo, hi = groups[g]
        block = mean.at[lo:hi, pl.ds(row_of(me, j, n_mem, width), 1)]
        return send(block, block, mean_send.at[n, p], mean_recv.at[n, p], lax.rem(me + p, n_mem))

    def merge(u):
        (lo, hi), (low, high) = units[u]
        if low == high:
            return
        for copy in part_copies[u]:
            copy.wait_recv()
        for j in range(low, high):
            if u == 0:
                logs = [logs_out[me, j]] + [logs_in[p, j] for p in range(1, n_mem)]
                best = functools.reduce(jnp.maximum, logs)
                expo = [jnp.exp(value - best) for value in logs]
                scale = 1.0 / functools.reduce(jnp.add, expo)
                for p in range(n_mem):
                    share_class[p, j] = expo[p] * scale
                for p in range(n_mem):
                    share[p, j] = expand(lambda i, h: share_class[p, j, h, pl.ds(i, 1)])
            weights = [share[p, j] for p in range(n_mem)]
            for k in range(lo, hi):
                total = weights[0] * part[me, k, j]
                for p in range(1, n_mem):
                    total = total + weights[p] * inbox[p, k, j]
                mean[order[k], row_of(me, j, n_mem, width)] = total
        for piece in pieces[u]:
            for p in range(1, n_mem):
                mean_copies.append(send_mean(piece, p))

    def late_winds():
        for copy in winds_halo:
            copy.wait_recv()
        at_rows(step_one, beyond, groups[1])
        at_rows(step_two, edges, groups[1])
        spread(2)

    def late_rest():
        for copies, span_m in zip(rest_halos, late_spans):
            for copy in copies:
                copy.wait_recv()
            at_rows(step_one, beyond + edges, groups[2], *span_m)
            at_rows(step_two, edges + inside, groups[2], *span_m)
        spread(3)

    spread(0)
    spread(1)
    late_rest()
    merge(0)
    late_winds()
    merge(1)
    merge(3)
    merge(2)

    for copy in mean_copies:
        copy.wait_recv()
    halos = sum(first_halos, []) + winds_halo + sum(rest_halos, [])
    for copy in halos + sum(img_copies, []) + sum(part_copies, []) + mean_copies:
        copy.wait_send()


def blend(adv, mean, out, staged, sems):
    members, fields = adv.shape[:2]
    copies = []
    for m in range(members):
        for f in range(fields):
            staged[m, f] = adv[m, f] + blend_share * (mean[f] - adv[m, f])
            copy = pltpu.make_async_copy(staged.at[m, f], out.at[m, f], sems.at[m, f])
            copy.start()
            copies.append(copy)
    for copy in copies:
        copy.wait()


def local(n_mem, n_space, state, diffusion, radius, obs_cells, obs_count, obs_value, obs_error):
    members, fields, width, levels, lat = state.shape
    sites_max = obs_cells.shape[1]
    dims = (members, fields, width, levels, lat, sites_max)
    each = width // n_mem
    chunks = lat // lanes
    n_radii = len(radius_range(width))
    slots = -(-n_radii // sublanes) * sublanes
    n_pieces = 3 * each
    dma = pltpu.SemaphoreType.DMA

    def vmem(*shape):
        return pltpu.VMEM(shape, jnp.float32)

    small = (diffusion, radius, obs_cells, obs_count, obs_value, obs_error)
    held = [
        value if value.size == 1 else pltpu.with_memory_space_constraint(value, pltpu.HBM)
        for value in (state, *small)
    ]
    hbm = pl.BlockSpec(memory_space=pltpu.HBM)
    adv, mean = pl.pallas_call(
        functools.partial(kernel, n_mem, n_space, dims),
        out_shape=[
            pltpu.VMEM(state.shape, jnp.float32),
            pltpu.VMEM(state.shape[1:], jnp.float32),
        ],
        in_specs=[hbm] * 7,
        out_specs=[pl.BlockSpec(memory_space=pltpu.VMEM)] * 2,
        scratch_shapes=[pltpu.SMEM(value.shape, value.dtype) for value in small]
        + [
            vmem(members, fields, width + 4, levels, lat),
            vmem(members, fields, width + 2, levels, lat),
            vmem(3, width, lat),
            vmem(members, chunks, 3 * width, lanes),
            vmem(width - 1, members, chunks, 3 * width, lanes),
            vmem(members, n_radii, chunks, width, lanes),
            vmem(members, width, levels, lat),
            vmem(n_mem, fields, each, levels, lat),
            vmem(n_mem, fields, each, levels, lat),
            vmem(n_mem, each, chunks, slots, lanes),
            vmem(n_mem, each, chunks, slots, lanes),
            vmem(n_mem, each, chunks, slots, lanes),
            vmem(n_mem, each, levels, lat),
            dma((len(small),)),
            dma,
            dma((4, members, 2)),
            dma((4, members, 2)),
            dma((members, 2)),
            dma((members, 2)),
            dma((4, n_mem)),
            dma((4, n_mem)),
            dma((n_mem,)),
            dma((n_mem,)),
            dma((n_pieces, n_mem)),
            dma((n_pieces, n_mem)),
        ],
        compiler_params=pltpu.CompilerParams(
            collective_id=0, has_side_effects=True, vmem_limit_bytes=24 * 2**20
        ),
    )(*held)
    return pl.pallas_call(
        blend,
        out_shape=jax.ShapeDtypeStruct(state.shape, jnp.float32),
        in_specs=[pl.BlockSpec(memory_space=pltpu.VMEM)] * 2,
        out_specs=pl.BlockSpec(memory_space=pltpu.HBM),
        scratch_shapes=[vmem(*state.shape), dma((members, fields))],
        compiler_params=pltpu.CompilerParams(vmem_limit_bytes=16 * 2**20),
    )(*[pltpu.with_memory_space_constraint(value, pltpu.VMEM) for value in (adv, mean)])


def solution(mesh):
    return jax.shard_map(
        functools.partial(local, mesh.shape["mem"], mesh.shape["space"]),
        mesh=mesh,
        in_specs=(
            P("mem", None, "space", None, None),
            P(),
            P(),
            P("space", None),
            P("space"),
            P("space", None),
            P("space", None),
        ),
        out_specs=P("mem", None, "space", None, None),
        check_vma=False,
    )
```
